32 devices in a mesh: grp: 2 (over y), row: 4 (over x, core), col: 4 (over z).
Axes of the slice: x: 2, y: 2, z: 4, core: 2. Of those that a mesh axis runs over, the one named last changes fastest.
Arguments:
- factor: float32 [8, 4, 768, 768], P(('grp', 'row'), 'col'), parts along dimension 0
- rhs: float32 [8, 768, 64], P(('grp', 'row')), parts along dimension 0, may hold values from -6 to 6
- pattern: int32 [8, 4], P('grp'), parts along dimension 0, may hold values from 0 to 1, as said below
Outputs:
- solution: float32 [8, 768, 64], P(('grp', 'col'), 'row'), parts along dimension 0
The draws below stay inside these ranges and needn't reach their ends.
There are 2 independent parts, one for each index of `grp`. The reference program is written for one: setup_inputs(seed, part) draws one part's arguments, and reference() takes and returns one part's arrays. A program takes and returns all parts, laid end to end along the dimension named above; each array names one. Nothing has to cross between parts.
Inputs may be any that keep to these rules, and one draw needn't show every extreme that they name: pattern[i, j] = 1 only where j < i; the blocks form an elimination tree in which every block but the last has exactly one parent p > j with pattern[p, j] = 1, and pattern[i, j] = 1 only where i is an ancestor of j; every chain of blocks linked by pattern has at most 4 blocks and some chain has exactly 4.
All inputs are finite; a program needn't handle non-finite values.
Results may differ from the reference program's by a relative error of at most 0.0001.
Values sent between devices are 32-bit elements; how exact they have to be, the bound alone decides.
A program may use at most 64 MiB of HBM per device.

```python
import jax
import jax.numpy as jnp
from jax import lax

TILE = 768
RHS = 64
BLOCKS = 4
LEVELS = 4


def draw_factor(key, part):
    key_base, key_diag = jax.random.split(jax.random.fold_in(key, 11))
    shape_all = (BLOCKS, BLOCKS, TILE, TILE)
    base = jax.random.normal(key_base, shape_all, jnp.float32)
    diag_values = jnp.exp(jax.random.uniform(key_diag, (BLOCKS, 1, TILE, 1), jnp.float32, jnp.log(0.5), jnp.log(2.0)))
    identity = jnp.eye(TILE, dtype=jnp.float32)
    on_diagonal = (jnp.arange(BLOCKS)[:, None] == jnp.arange(BLOCKS)[None, :])[:, :, None, None]
    dominant = base * (0.5 / jnp.sqrt(TILE * 1.0)) + diag_values * identity
    return jnp.where(on_diagonal, dominant, base / jnp.sqrt(8.0 * TILE))


def draw_pattern(key, part):
    key_parent, key_bits = jax.random.split(jax.random.fold_in(key, 7))
    indices = jnp.arange(BLOCKS, dtype=jnp.int32)
    spine_start = BLOCKS - LEVELS
    leaf_parent = spine_start + jax.random.randint(key_parent, (BLOCKS,), 1, LEVELS, dtype=jnp.int32)
    parents = jnp.where(indices >= spine_start, indices + 1, leaf_parent)
    position = jnp.where(indices >= spine_start, indices - spine_start, leaf_parent - spine_start - 1)
    ancestor = (indices[:, None] >= spine_start) & (indices[:, None] - spine_start > position[None, :])
    random_bits = jax.random.randint(key_bits, (BLOCKS, BLOCKS), 0, 2, dtype=jnp.int32)
    is_parent = indices[:, None] == parents[None, :]
    return jnp.where(ancestor, jnp.where(is_parent, 1, random_bits), 0).astype(jnp.int32)


def steps_of(own_key, shape, pieces, smallest, high):
    loudness = 1.0
    for axis_at, parts in pieces:
        draws = jax.random.uniform(jax.random.fold_in(jax.random.fold_in(own_key, 6), axis_at), (parts,), jnp.float32, smallest / len(pieces), high / len(pieces))
        loudness = loudness * jnp.repeat(jnp.exp(draws), shape[axis_at] // parts).reshape((-1,) + (1,) * (len(shape) - 1 - axis_at))
    return loudness


def normal_values(stream_key, shape, deviation, reach, cuts=(), kind=jnp.bfloat16):
    level = steps_of(stream_key, shape, cuts, -0.22, 0.18) if cuts else 1.0
    entries = jax.random.normal(stream_key, shape, jnp.float32) * deviation * level
    return jnp.minimum(jnp.maximum(entries, -reach), reach).astype(kind)


def setup_inputs(seed: int = 0, part: int = 0) -> dict:
    key_list = jax.random.split(jax.random.key(seed), 4)
    part_keys = jax.random.split(jax.random.fold_in(key_list[3], part), 4)
    return {
        "factor": draw_factor(jax.random.fold_in(jax.random.fold_in(key_list[3], part), 71), part),
        "rhs": normal_values(part_keys[1], (BLOCKS, TILE, RHS), 1.0, 6.0, ((0, 4),), jnp.float32),
        "pattern": draw_pattern(jax.random.fold_in(jax.random.fold_in(key_list[3], part), 71), part),
    }


def reference(factor, rhs, pattern):
    solved = jnp.zeros((BLOCKS, TILE, RHS), jnp.float32)
    for block_index in range(BLOCKS):
        weights = (pattern[block_index] == 1).astype(jnp.float32)
        carried = jnp.einsum("jab,jbr->ar", factor[block_index], solved * weights[:, None, None], precision=lax.Precision.HIGHEST)
        answer = jnp.dot(factor[block_index, block_index], rhs[block_index] - carried, precision=lax.Precision.HIGHEST, preferred_element_type=jnp.float32)
        solved = solved.at[block_index].set(answer)
    return solved
```

```python
import functools

import jax
import jax.numpy as jnp
from jax import lax
from jax.experimental import pallas as pl
from jax.experimental.pallas import tpu as pltpu
from jax.sharding import PartitionSpec as P

MESH = pl.DeviceIdType.MESH
BF = jnp.bfloat16
F32 = jnp.float32


def split(value):
    lead = value.astype(BF)
    rest = (value - lead.astype(F32)).astype(BF)
    return jnp.concatenate([lead, rest], axis=0), lead


def product(pair, hi, lo, cols):
    both, lead = pair
    rows = lead.shape[0]
    part = jnp.dot(both, hi[:, cols], preferred_element_type=F32)
    rest = jnp.dot(lead, lo[:, cols], preferred_element_type=F32)
    return part[:rows] + part[rows:] + rest


def turn(source, start, count, hi, lo, at, keep):
    def put(rows, cols):
        full = source[rows, :].T * keep
        lead = full.astype(BF)
        hi[:, cols] = lead
        lo[:, cols] = (full - lead.astype(F32)).astype(BF)

    if count % 128:
        put(slice(start, start + count), slice(at, at + count))
        return

    def one(t, carry):
        put(
            pl.ds(pl.multiple_of(start + t * 128, 128), 128),
            pl.ds(pl.multiple_of(at + t * 128, 128), 128),
        )
        return carry

    lax.fori_loop(0, count // 128, one, 0)


def kernel(
    n, size, rhs_count, step, groups, own, slot,
    factor, rhs, pattern, out,
    links, a32, b32, h32, ahi, alo, bhi, blo, mhi, mlo, hhi, hlo,
    right, right_a, xbuf, resid, pa_in, pa_out, pb_in, pb_out, piece, tail,
    a_sem, r_sem, l_sem, ship_send, ship_recv, rb_send, rb_recv, x_send, x_recv,
    pa_send, pa_recv, pb_send, pb_recv, s_send, s_recv, t_send, d_send, d_recv,
):
    r = lax.axis_index("row")
    c = lax.axis_index("col")
    chunks = size // step
    ng = rhs_count // groups
    early = n // 2
    odd = lax.rem(r, 2) == 1
    even = jnp.logical_not(odd)
    port = r + 1 - lax.rem(r, 2)
    first = (r == 0) & (c == 0)
    second = (r == 1) & (c == 0)
    interior = odd & (c < r - 1)
    above = odd & (c == r - 1)
    above_late = above & (r > 1)
    below = odd & (c == r)
    final = below & (r == n - 1)
    helper = above & (r == n - 1)
    below_mid = below & (r < n - 1)
    ships = even & (c <= r)
    works = odd & (c <= r)
    last_col = c == n - 1
    source = 2 * (c // 2) + 1
    upstream = c > port

    def load(k):
        rows = pl.ds(k * step, step)
        return pltpu.make_async_copy(factor.at[0, 0, rows, :], a32.at[rows, :], a_sem.at[k])

    def load_right():
        return pltpu.make_async_copy(rhs.at[0], right, r_sem)

    def load_links():
        return pltpu.make_async_copy(pattern, links, l_sem)

    @pl.when(first | works)
    def _():
        for k in range(chunks):
            load(k).start()
        load_right().start()

    @pl.when(works)
    def _():
        load_links().start()

    barrier = pltpu.get_barrier_semaphore()

    def hello(row, col):
        pl.semaphore_signal(barrier, inc=1, device_id={"row": row, "col": col}, device_id_type=MESH)

    @pl.when(odd & (c <= r - 1))
    def _():
        hello(r - 1, c)

    @pl.when(interior)
    def _():
        hello(r - 2, c)

    @pl.when(works & (c > 0))
    def _():
        hello(r, c - 1)

    @pl.when(helper)
    def _():
        hello(n - 1, n - 1)

    @pl.when(upstream & last_col & (r < early))
    def _():
        hello(n - 1, n - 2)

    @pl.when(upstream & jnp.logical_not(last_col & (r < early)))
    def _():
        hello(source, c)

    @pl.when(even & (c <= r + 1) & jnp.logical_not(first))
    def _():
        hello(r + 1, c)

    def one_if(flag):
        return jnp.where(flag, 1, 0)

    @pl.when(ships)
    def _():
        pl.semaphore_wait(barrier, 1)

    def meet():
        count = one_if(jnp.logical_not(second)) + one_if(r + 2 < n) + one_if(c < r)
        count += jnp.where((above | below) & jnp.logical_not(final), r - 1, 0)
        count += jnp.where(final, n - 2 - early + 1, 0) + jnp.where(helper, early, 0)
        pl.semaphore_wait(barrier, count)

    def ship(k, row):
        rows = pl.ds(k * step, step)
        return pltpu.make_async_remote_copy(
            src_ref=factor.at[0, 0, rows, :], dst_ref=b32.at[rows, :],
            send_sem=ship_send.at[k], recv_sem=ship_recv.at[k],
            device_id={"row": row}, device_id_type=MESH,
        )

    def ship_right(row):
        return pltpu.make_async_remote_copy(
            src_ref=rhs.at[0], dst_ref=right_a, send_sem=rb_send, recv_sem=rb_recv,
            device_id={"row": row}, device_id_type=MESH,
        )

    def group(g):
        return pl.ds(pl.multiple_of(g * ng, ng), ng)

    def lanes(m):
        return slice(m * step, (m + 1) * step)

    def x_whole(g, row):
        return pltpu.make_async_remote_copy(
            src_ref=xbuf.at[group(g), :], dst_ref=xbuf.at[group(g), :],
            send_sem=x_send.at[g, 0], recv_sem=x_recv.at[g, 0],
            device_id={"row": row}, device_id_type=MESH,
        )

    def x_chunk(g, m, row):
        return pltpu.make_async_remote_copy(
            src_ref=xbuf.at[group(g), lanes(m)], dst_ref=xbuf.at[group(g), lanes(m)],
            send_sem=x_send.at[g, m], recv_sem=x_recv.at[g, m],
            device_id={"row": row}, device_id_type=MESH,
        )

    def pa_chunk(g, m, col):
        return pltpu.make_async_remote_copy(
            src_ref=pa_out.at[group(g), lanes(m)], dst_ref=pa_in.at[group(g), lanes(m)],
            send_sem=pa_send.at[g, m], recv_sem=pa_recv.at[g, m],
            device_id={"col": col}, device_id_type=MESH,
        )

    def pb_chunk(g, m, col):
        return pltpu.make_async_remote_copy(
            src_ref=pb_out.at[group(g), lanes(m)], dst_ref=pb_in.at[group(g), lanes(m)],
            send_sem=pb_send.at[g, m], recv_sem=pb_recv.at[g, m],
            device_id={"col": col}, device_id_type=MESH,
        )

    def pb_whole(g, col):
        return pltpu.make_async_remote_copy(
            src_ref=pb_out.at[group(g), :], dst_ref=pb_in.at[group(g), :],
            send_sem=pb_send.at[g, 0], recv_sem=pb_recv.at[g, 0],
            device_id={"col": col}, device_id_type=MESH,
        )

    def s_copy(k):
        return pltpu.make_async_remote_copy(
            src_ref=piece.at[k], dst_ref=out.at[0], send_sem=s_send.at[k], recv_sem=s_recv.at[0],
            device_id={"row": k}, device_id_type=MESH,
        )

    def h_copy(k):
        return pltpu.make_async_remote_copy(
            src_ref=tail.at[k], dst_ref=out.at[0], send_sem=t_send.at[k, 0], recv_sem=s_recv.at[0],
            device_id={"row": k, "col": n - 1}, device_id_type=MESH,
        )

    def t_copy(k, g):
        return pltpu.make_async_remote_copy(
            src_ref=tail.at[k, group(g), :], dst_ref=out.at[0, group(g), :],
            send_sem=t_send.at[k, g], recv_sem=s_recv.at[g],
            device_id={"row": k}, device_id_type=MESH,
        )

    def d_copy(k):
        rows = pl.ds(k * own, own)
        return pltpu.make_async_remote_copy(
            src_ref=factor.at[0, 0, rows, :], dst_ref=h32.at[rows, :],
            send_sem=d_send.at[k], recv_sem=d_recv.at[k],
            device_id={"col": n - 2}, device_id_type=MESH,
        )

    def each(body):
        def step_of(g, carry):
            body(g)
            return carry

        lax.fori_loop(0, groups, step_of, 0)

    def prepare(k, hi, lo, keep):
        load(k).wait()
        turn(a32, k * step, step, hi, lo, k * step, keep)

    def receive(k, keep):
        ship(k, r - 1).wait_recv()
        turn(b32, k * step, step, ahi, alo, k * step, keep)

    def slices():
        for k in range(n):
            @pl.when((k < r) & jnp.logical_not(second) & ((k == r - 1) | (c >= r - 1)))
            def _():
                piece[k] = xbuf[:, k * own:(k + 1) * own]
                s_copy(k).start()

            @pl.when(k == r)
            def _():
                out[0] = xbuf[:, k * own:(k + 1) * own]

    @pl.when(ships & jnp.logical_not(first))
    def _():
        for k in range(chunks):
            ship(k, r + 1).start()

        @pl.when(c == r)
        def _():
            ship_right(r + 1).start()

    @pl.when(first)
    def _():
        load_right().wait()
        pair = split(right[...])
        for m in range(chunks):
            prepare(m, bhi, blo, jnp.float32(1.0))
            xbuf[:, lanes(m)] = product(pair, bhi, blo, lanes(m))
        for g in range(groups):
            x_whole(g, 1).start()
        out[0] = xbuf[:, :own]

    @pl.when(works)
    def _():
        load_links().wait()

        @pl.when(final)
        def _():
            meet()
            for k in range(early):
                d_copy(k).start()

        load_right().wait()
        keep_own = jnp.where(below | (links[r, c] == 1), 1.0, 0.0).astype(F32)
        keep_up = jnp.where(above | (links[r - 1, c] == 1), 1.0, 0.0).astype(F32)

        @pl.when(jnp.logical_not(final))
        def _():
            for k in range(chunks):
                prepare(k, bhi, blo, keep_own)

        @pl.when(final)
        def _():
            for k in range(chunks):
                load(k).wait()
            for k in range(early, n):
                turn(a32, k * own, own, bhi, blo, (k - early) * slot, keep_own)

        @pl.when(interior | above_late)
        def _():
            for k in range(chunks):
                receive(k, keep_up)

        @pl.when(jnp.logical_not(final))
        def _():
            meet()

    @pl.when(second)
    def _():
        def body(g):
            x_whole(g, 0).wait_recv()
            if n > 2:
                x_whole(g, 3).start()
            pair = split(xbuf[group(g), :])
            for m in range(chunks):
                pb_out[group(g), lanes(m)] = product(pair, bhi, blo, lanes(m))
                pb_chunk(g, m, 1).start()

        each(body)

    @pl.when(below_mid)
    def _():
        def body(g):
            for m in range(chunks):
                pb_chunk(g, m, c - 1).wait_recv()
            pair = split(right[group(g), :] - pb_in[group(g), :])
            for m in range(chunks):
                xbuf[group(g), lanes(m)] = product(pair, bhi, blo, lanes(m))
                x_chunk(g, m, r + 2).start()

        each(body)

    @pl.when(interior)
    def _():
        def body(g):
            @pl.when(lax.rem(c, 2) == 0)
            def _():
                x_whole(g, r - 2).wait_recv()

                @pl.when(r + 2 < n)
                def _():
                    x_whole(g, r + 2).start()

            @pl.when(lax.rem(c, 2) == 1)
            def _():
                for m in range(chunks):
                    x_chunk(g, m, r - 2).wait_recv()

                    @pl.when(r + 2 < n)
                    def _():
                        x_chunk(g, m, r + 2).start()

            @pl.when(c > 0)
            def _():
                for m in range(chunks):
                    pa_chunk(g, m, c - 1).wait_recv()

            pair = split(xbuf[group(g), :])
            scale = jnp.where(c > 0, 1, 0)
            for m in range(chunks):
                part = product(pair, ahi, alo, lanes(m))
                pa_out[group(g), lanes(m)] = part

                @pl.when(scale > 0)
                def _():
                    pa_out[group(g), lanes(m)] = part + pa_in[group(g), lanes(m)]

                pa_chunk(g, m, c + 1).start()

        each(body)
        pair = split(xbuf[...])
        for m in range(chunks):
            pb_out[:, lanes(m)] = product(pair, bhi, blo, lanes(m))

        def send(g):
            @pl.when(c > 0)
            def _():
                pb_whole(g, c - 1).wait_recv()
                pb_out[group(g), :] += pb_in[group(g), :]

            pb_whole(g, c + 1).start()

        each(send)

    @pl.when(above_late)
    def _():
        for m in range(chunks):
            def rows_of(q, carry):
                rows = pl.ds(pl.multiple_of(q * step, step), step)
                part = jnp.dot(ahi[rows, :], bhi[:, lanes(m)], preferred_element_type=F32)
                part += jnp.dot(alo[rows, :], bhi[:, lanes(m)], preferred_element_type=F32)
                part += jnp.dot(ahi[rows, :], blo[:, lanes(m)], preferred_element_type=F32)
                lead = part.astype(BF)
                mhi[rows, lanes(m)] = lead
                mlo[rows, lanes(m)] = (part - lead.astype(F32)).astype(BF)
                return carry

            lax.fori_loop(0, chunks, rows_of, 0)
        ship_right(r - 1).wait_recv()

        def body(g):
            for m in range(chunks):
                pa_chunk(g, m, c - 1).wait_recv()
            value = right_a[group(g), :] - pa_in[group(g), :]
            resid[group(g), :] = value
            pair = split(value)
            for m in range(chunks):
                pb_out[group(g), lanes(m)] = product(pair, mhi, mlo, lanes(m))

        each(body)
        pair = split(resid[...])
        for m in range(chunks):
            xbuf[:, lanes(m)] = product(pair, ahi, alo, lanes(m))

        @pl.when(r + 2 < n)
        def _():
            for g in range(groups):
                x_whole(g, r + 2).start()

        def send(g):
            pb_whole(g, c - 1).wait_recv()
            pb_out[group(g), :] += pb_in[group(g), :]
            for m in range(chunks):
                pb_chunk(g, m, c + 1).start()

        each(send)

        @pl.when(helper)
        def _():
            for k in range(early):
                d_copy(k).wait_recv()
                turn(h32, k * own, own, hhi, hlo, k * slot, jnp.float32(1.0))
            pair = split(right[...] - pb_out[...])
            for k in range(early):
                tail[k] = product(pair, hhi, hlo, slice(k * slot, (k + 1) * slot))[:, :own]
                h_copy(k).start()

    @pl.when(works & jnp.logical_not(final))
    def _():
        slices()

    @pl.when(final)
    def _():
        def body(g):
            for m in range(chunks):
                pb_chunk(g, m, c - 1).wait_recv()
            pair = split(right[group(g), :] - pb_in[group(g), :])
            for k in range(early, n):
                value = product(pair, bhi, blo, slice((k - early) * slot, (k - early + 1) * slot))
                if k == n - 1:
                    out[0, group(g), :] = value[:, :own]
                else:
                    tail[k, group(g), :] = value[:, :own]
                    t_copy(k, g).start()

        each(body)

    needs = jnp.logical_not(first) & jnp.logical_not(works)

    @pl.when(needs & last_col & (r >= early))
    def _():
        for g in range(groups):
            t_copy(n - 1, g).wait_recv()

    @pl.when(needs & jnp.logical_not(last_col & (r >= early)))
    def _():
        s_copy(0).wait_recv()

    @pl.when(ships & jnp.logical_not(first))
    def _():
        for k in range(chunks):
            ship(k, r + 1).wait_send()

        @pl.when(c == r)
        def _():
            ship_right(r + 1).wait_send()

    x_by_group = (lax.rem(c, 2) == 0) & (first | (works & (r + 2 < n)))

    @pl.when(x_by_group)
    def _():
        for g in range(groups):
            x_whole(g, r + 1).wait_send()

    @pl.when(works & (lax.rem(c, 2) == 1) & (r + 2 < n))
    def _():
        for g in range(groups):
            for m in range(chunks):
                x_chunk(g, m, r + 1).wait_send()

    @pl.when(interior)
    def _():
        for g in range(groups):
            pb_whole(g, c + 1).wait_send()
            for m in range(chunks):
                pa_chunk(g, m, c + 1).wait_send()

    @pl.when(above)
    def _():
        for g in range(groups):
            for m in range(chunks):
                pb_chunk(g, m, c + 1).wait_send()

    for k in range(n):
        @pl.when(
            works & jnp.logical_not(final) & jnp.logical_not(second) & (k < r) & ((k == r - 1) | (c >= r - 1))
        )
        def _():
            s_copy(k).wait_send()

    @pl.when(helper)
    def _():
        for k in range(early):
            h_copy(k).wait_send()

    @pl.when(final)
    def _():
        for k in range(early):
            d_copy(k).wait_send()
        for k in range(early, n - 1):
            for g in range(groups):
                t_copy(k, g).wait_send()


def local(n, factor, rhs, pattern):
    size, columns = rhs.shape[1], rhs.shape[2]
    step = 256 if size % 256 == 0 else size
    chunks = size // step
    groups = 4
    own = size // n
    slot = (own + 127) // 128 * 128
    early = n // 2
    dma = pltpu.SemaphoreType.DMA
    vm = pltpu.VMEM
    wide = max(size, (n - early) * slot)
    solved = pl.pallas_call(
        functools.partial(kernel, n, size, columns, step, groups, own, slot),
        out_shape=jax.ShapeDtypeStruct((1, columns, own), F32),
        in_specs=[pl.BlockSpec(memory_space=pltpu.HBM)] * 3,
        out_specs=pl.BlockSpec(memory_space=pltpu.VMEM),
        scratch_shapes=[
            pltpu.SMEM(pattern.shape, jnp.int32),
            vm((size, size), F32), vm((size, size), F32), vm((early * own, size), F32),
            vm((size, size), BF), vm((size, size), BF),
            vm((size, wide), BF), vm((size, wide), BF),
            vm((size, size), BF), vm((size, size), BF),
            vm((size, early * slot), BF), vm((size, early * slot), BF),
            *[vm((columns, size), F32)] * 8,
            vm((n, columns, own), F32), vm((n, columns, own), F32),
            dma((chunks,)), dma, dma, dma((chunks,)), dma((chunks,)), dma, dma,
            dma((groups, chunks)), dma((groups, chunks)),
            dma((groups, chunks)), dma((groups, chunks)),
            dma((groups, chunks)), dma((groups, chunks)),
            dma((n,)), dma((groups,)), dma((n, groups)),
            dma((early,)), dma((early,)),
        ],
        compiler_params=pltpu.CompilerParams(
            collective_id=0, has_side_effects=True, vmem_limit_bytes=40 * 1024 * 1024
        ),
    )(*[pltpu.with_memory_space_constraint(v, pltpu.HBM) for v in (factor, jnp.swapaxes(rhs, 1, 2), pattern)])
    return jnp.swapaxes(solved, 1, 2)


def solution(mesh):
    in_specs = (P(("grp", "row"), "col", None, None), P(("grp", "row"), None, None), P("grp", None))
    out_specs = P(("grp", "col"), "row", None)
    return jax.shard_map(
        functools.partial(local, mesh.shape["row"]),
        mesh=mesh, in_specs=in_specs, out_specs=out_specs, check_vma=False,
    )
```

```python
import functools

import jax
import jax.numpy as jnp
from jax import lax
from jax.experimental import pallas as pl
from jax.experimental.pallas import tpu as pltpu
from jax.sharding import PartitionSpec as P

MESH = pl.DeviceIdType.MESH
BF = jnp.bfloat16
F32 = jnp.float32


def split(value):
    lead = value.astype(BF)
    rest = (value - lead.astype(F32)).astype(BF)
    return jnp.concatenate([lead, rest], axis=0), lead


def product(pair, hi, lo, cols):
    both, lead = pair
    rows = lead.shape[0]
    part = jnp.dot(both, hi[:, cols], preferred_element_type=F32)
    rest = jnp.dot(lead, lo[:, cols], preferred_element_type=F32)
    return part[:rows] + part[rows:] + rest


def turn(source, start, count, hi, lo, at, keep):
    width = 128 if count % 128 == 0 else count
    for t in range(0, count, width):
        full = source[start + t:start + t + width, :].T * keep
        lead = full.astype(BF)
        hi[:, at + t:at + t + width] = lead
        lo[:, at + t:at + t + width] = (full - lead.astype(F32)).astype(BF)


def across(pair, block):
    both, lead = pair
    rows = lead.shape[0]
    dims = (((1,), (1,)), ((), ()))
    top = block.astype(BF)
    low = (block - top.astype(F32)).astype(BF)
    part = lax.dot_general(both, top, dims, preferred_element_type=F32)
    rest = lax.dot_general(lead, low, dims, preferred_element_type=F32)
    return part[:rows] + part[rows:] + rest


def kernel(
    n, size, rhs_count, step, groups, own, slot,
    factor, rhs, pattern, out,
    links, a32, b32, h32, ahi, alo, bhi, blo, mhi, mlo, hhi, hlo,
    right, right_a, xbuf, resid, pa_in, pa_out, pb_in, pb_out, piece, tail,
    a_sem, r_sem, l_sem, ship_send, ship_recv, rb_send, rb_recv, x_send, x_recv,
    pa_send, pa_recv, pb_send, pb_recv, s_send, s_recv, t_send, d_send, d_recv, rr_send, rr_recv,
):
    r = lax.axis_index("row")
    c = lax.axis_index("col")
    chunks = size // step
    ng = rhs_count // groups
    early = n // 2
    direct = early // 2
    parts = 3 if own % 24 == 0 else 1
    third = own // parts
    half = rhs_count // 2
    odd = lax.rem(r, 2) == 1
    even = jnp.logical_not(odd)
    port = r + 1 - lax.rem(r, 2)
    first = (r == 0) & (c == 0)
    second = (r == 1) & (c == 0)
    interior = odd & (c < r - 1)
    above = odd & (c == r - 1)
    above_late = above & (r > 1)
    below = odd & (c == r)
    final = below & (r == n - 1)
    helper = above & (r == n - 1)
    below_mid = below & (r < n - 1)
    relay = (r == n - 3) & (c == n - 1)
    ships = even & (c <= r)
    late = even & (c == r) & (r > 0)
    works = odd & (c <= r)
    last_col = c == n - 1
    upstream = c > port

    def load(k):
        rows = pl.ds(k * step, step)
        return pltpu.make_async_copy(factor.at[0, 0, rows, :], a32.at[rows, :], a_sem.at[k])

    def load_right():
        return pltpu.make_async_copy(rhs.at[0], right, r_sem)

    def load_links():
        return pltpu.make_async_copy(pattern, links, l_sem)

    @pl.when(works)
    def _():
        load_links().start()

    @pl.when(first | works)
    def _():
        load_right().start()

    @pl.when(first | works | late)
    def _():
        for k in range(chunks):
            load(k).start()

    barrier = pltpu.get_barrier_semaphore()

    def hello(row, col):
        pl.semaphore_signal(barrier, inc=1, device_id={"row": row, "col": col}, device_id_type=MESH)

    @pl.when(odd & (c <= r - 1))
    def _():
        hello(r - 1, c)

    @pl.when(interior)
    def _():
        hello(jnp.where((c == r - 3) & (c > 0), r - 3, r - 2), c)

    @pl.when(works & (c > 0))
    def _():
        hello(r, c - 1)

    @pl.when(helper)
    def _():
        hello(n - 1, n - 1)
        hello(n - 3, n - 1)

    @pl.when(relay)
    def _():
        hello(n - 1, n - 1)

    @pl.when(upstream & last_col & (r < early))
    def _():
        hello(n - 1, n - 2)

    @pl.when(upstream & jnp.logical_not(last_col & (r < early)))
    def _():
        hello(c, c)

    @pl.when(even & (c <= r + 1) & jnp.logical_not(first))
    def _():
        hello(r + 1, c)

    def one_if(flag):
        return jnp.where(flag, 1, 0)

    @pl.when(ships)
    def _():
        pl.semaphore_wait(barrier, 1 + jnp.where(late, r + one_if(r + 3 < n), 0))

    def meet():
        count = one_if(jnp.logical_not(second)) + one_if((r + 2 < n) & jnp.logical_not(above_late)) + one_if(c < r)
        count += jnp.where(below_mid, r - 1, 0)
        count += jnp.where(final, n - early, 0) + jnp.where(helper, early, 0)
        pl.semaphore_wait(barrier, count)

    def ship(k, row):
        rows = pl.ds(k * step, step)
        return pltpu.make_async_remote_copy(
            src_ref=factor.at[0, 0, rows, :], dst_ref=b32.at[rows, :],
            send_sem=ship_send.at[k], recv_sem=ship_recv.at[k],
            device_id={"row": row}, device_id_type=MESH,
        )

    def ship_right(row):
        return pltpu.make_async_remote_copy(
            src_ref=rhs.at[0], dst_ref=right_a, send_sem=rb_send, recv_sem=rb_recv,
            device_id={"row": row}, device_id_type=MESH,
        )

    def group(g):
        return pl.ds(pl.multiple_of(g * ng, ng), ng)

    def lanes(m):
        return slice(m * step, (m + 1) * step)

    def x_whole(g, row):
        return pltpu.make_async_remote_copy(
            src_ref=xbuf.at[group(g), :], dst_ref=xbuf.at[group(g), :],
            send_sem=x_send.at[g, 0], recv_sem=x_recv.at[g, 0],
            device_id={"row": row}, device_id_type=MESH,
        )

    def x_chunk(g, m, row):
        return pltpu.make_async_remote_copy(
            src_ref=xbuf.at[group(g), lanes(m)], dst_ref=xbuf.at[group(g), lanes(m)],
            send_sem=x_send.at[g, m], recv_sem=x_recv.at[g, m],
            device_id={"row": row}, device_id_type=MESH,
        )

    def pa_chunk(g, m, col):
        return pltpu.make_async_remote_copy(
            src_ref=pa_out.at[group(g), lanes(m)], dst_ref=pa_in.at[group(g), lanes(m)],
            send_sem=pa_send.at[g, m], recv_sem=pa_recv.at[g, m],
            device_id={"col": col}, device_id_type=MESH,
        )

    def pb_chunk(g, m, col):
        return pltpu.make_async_remote_copy(
            src_ref=pb_out.at[group(g), lanes(m)], dst_ref=pb_in.at[group(g), lanes(m)],
            send_sem=pb_send.at[g, m], recv_sem=pb_recv.at[g, m],
            device_id={"col": col}, device_id_type=MESH,
        )

    def pb_whole(g, col):
        return pltpu.make_async_remote_copy(
            src_ref=pb_out.at[group(g), :], dst_ref=pb_in.at[group(g), :],
            send_sem=pb_send.at[g, 0], recv_sem=pb_recv.at[g, 0],
            device_id={"col": col}, device_id_type=MESH,
        )

    def s_copy(k):
        return pltpu.make_async_remote_copy(
            src_ref=piece.at[k], dst_ref=out.at[0], send_sem=s_send.at[k], recv_sem=s_recv.at[0],
            device_id={"row": k}, device_id_type=MESH,
        )

    def h_copy(k, h):
        rows = pl.ds(h * half, half)
        return pltpu.make_async_remote_copy(
            src_ref=tail.at[k, rows, :], dst_ref=out.at[0, rows, :], send_sem=t_send.at[k, h], recv_sem=s_recv.at[h],
            device_id={"row": k, "col": n - 1}, device_id_type=MESH,
        )

    def t_copy(k, g):
        return pltpu.make_async_remote_copy(
            src_ref=tail.at[k, group(g), :], dst_ref=out.at[0, group(g), :],
            send_sem=t_send.at[k, g], recv_sem=s_recv.at[g],
            device_id={"row": k}, device_id_type=MESH,
        )

    def r_copy(g, row):
        return pltpu.make_async_remote_copy(
            src_ref=resid.at[group(g), :], dst_ref=resid.at[group(g), :],
            send_sem=rr_send.at[g], recv_sem=rr_recv.at[g],
            device_id={"row": row}, device_id_type=MESH,
        )

    def d_rows(k, q):
        return pl.ds(k * own + q * third, third)

    def d_copy(k, q):
        return pltpu.make_async_remote_copy(
            src_ref=factor.at[0, 0, d_rows(k, q), :], dst_ref=h32.at[d_rows(k, q), :],
            send_sem=d_send.at[k, q], recv_sem=d_recv.at[k, q],
            device_id={"row": n - 1 if k < direct else n - 3, "col": n - 2 if k < direct else n - 1},
            device_id_type=MESH,
        )

    def d_relay(k, q):
        return pltpu.make_async_remote_copy(
            src_ref=h32.at[d_rows(k, q), :], dst_ref=h32.at[d_rows(k, q), :],
            send_sem=d_send.at[k, q], recv_sem=d_recv.at[k, q],
            device_id={"row": n - 1, "col": n - 2}, device_id_type=MESH,
        )

    pieces = [(k, q) for k in range(early) for q in range(parts)]
    relayed = [(k, q) for k, q in pieces if k >= direct]

    def each(body):
        def step_of(g, carry):
            body(g)
            return carry

        lax.fori_loop(0, groups, step_of, 0)

    def rolled(pair, hi, lo, emit):
        before = None
        for m in range(chunks):
            part = product(pair, hi, lo, lanes(m))
            if m:
                emit(m - 1, before)
            before = part
        emit(chunks - 1, before)

    def prepare(k, hi, lo, keep):
        load(k).wait()
        turn(a32, k * step, step, hi, lo, k * step, keep)

    def receive(k, keep):
        ship(k, r - 1).wait_recv()
        turn(b32, k * step, step, ahi, alo, k * step, keep)

    def slices():
        for k in range(n):
            @pl.when((k < r) & jnp.logical_not(second) & ((k == r - 1) | (c == r)))
            def _():
                piece[k] = xbuf[:, k * own:(k + 1) * own]
                s_copy(k).start()

            @pl.when(k == r)
            def _():
                out[0] = xbuf[:, k * own:(k + 1) * own]

    @pl.when(ships & jnp.logical_not(first))
    def _():
        for k in range(chunks):
            ship(k, r + 1).start()

        @pl.when(c == r)
        def _():
            ship_right(r + 1).start()

    @pl.when(late)
    def _():
        for k in range(chunks):
            prepare(k, bhi, blo, jnp.float32(1.0))
        for g in range(groups):
            r_copy(g, r + 1).wait_recv()
        pair = split(resid[...])
        for m in range(chunks):
            xbuf[:, lanes(m)] = product(pair, bhi, blo, lanes(m))

        @pl.when(r + 3 < n)
        def _():
            for g in range(groups):
                x_whole(g, r + 3).start()

        for k in range(n):
            @pl.when((k < r + 2) & (k != r))
            def _():
                piece[k] = xbuf[:, k * own:(k + 1) * own]
                s_copy(k).start()

            @pl.when(k == r)
            def _():
                out[0] = xbuf[:, k * own:(k + 1) * own]

    @pl.when(first)
    def _():
        load_right().wait()
        pair = split(right[...])
        strip = 128 if step % 128 == 0 else step
        for m in range(chunks):
            load(m).wait()
            for t in range(m * step, (m + 1) * step, strip):
                xbuf[:, t:t + strip] = across(pair, a32[t:t + strip, :])
        for g in range(groups):
            x_whole(g, 1).start()
        out[0] = xbuf[:, :own]

    @pl.when(works)
    def _():
        load_links().wait()

        @pl.when(final)
        def _():
            meet()
            for q in range(parts):
                for k in range(early):
                    d_copy(k, q).start()

        load_right().wait()
        keep_own = jnp.where(below | (links[r, c] == 1), 1.0, 0.0).astype(F32)
        keep_up = jnp.where(above | (links[r - 1, c] == 1), 1.0, 0.0).astype(F32)

        @pl.when(jnp.logical_not(final))
        def _():
            for k in range(chunks):
                prepare(k, bhi, blo, keep_own)

        @pl.when(final)
        def _():
            for k in range(chunks):
                load(k).wait()
            for k in range(early, n):
                turn(a32, k * own, own, bhi, blo, (k - early) * slot, keep_own)

        @pl.when(interior | above_late)
        def _():
            for k in range(chunks):
                receive(k, keep_up)

        @pl.when(jnp.logical_not(final))
        def _():
            meet()

    @pl.when(relay)
    def _():
        pl.semaphore_wait(barrier, 1)
        for k, q in relayed:
            d_copy(k, q).wait_recv()
            d_relay(k, q).start()

    @pl.when(second)
    def _():
        def body(g):
            x_whole(g, 0).wait_recv()
            if n > 2:
                x_whole(g, 3).start()
            pair = split(xbuf[group(g), :])

            def emit(m, part):
                pb_out[group(g), lanes(m)] = part
                pb_chunk(g, m, 1).start()

            rolled(pair, bhi, blo, emit)

        each(body)

    @pl.when(below_mid)
    def _():
        def body(g):
            for m in range(chunks):
                pb_chunk(g, m, c - 1).wait_recv()
            pair = split(right[group(g), :] - pb_in[group(g), :])

            def emit(m, part):
                xbuf[group(g), lanes(m)] = part
                x_chunk(g, m, r + 2).start()

            rolled(pair, bhi, blo, emit)

        each(body)

    @pl.when(interior)
    def _():
        def body(g):
            @pl.when(lax.rem(c, 2) == 0)
            def _():
                x_whole(g, r - 2).wait_recv()

                @pl.when(r + 2 < n)
                def _():
                    x_whole(g, r + 2).start()

            @pl.when(lax.rem(c, 2) == 1)
            def _():
                for m in range(chunks):
                    x_chunk(g, m, r - 2).wait_recv()

                    @pl.when(r + 2 < n)
                    def _():
                        x_chunk(g, m, r + 2).start()

            @pl.when(c > 0)
            def _():
                for m in range(chunks):
                    pa_chunk(g, m, c - 1).wait_recv()

            pair = split(xbuf[group(g), :])

            def emit(m, part):
                pa_out[group(g), lanes(m)] = jnp.where(c > 0, part + pa_in[group(g), lanes(m)], part)
                pa_chunk(g, m, c + 1).start()

            rolled(pair, ahi, alo, emit)

        each(body)
        pair = split(xbuf[...])
        for m in range(chunks):
            pb_out[:, lanes(m)] = product(pair, bhi, blo, lanes(m))

        def send(g):
            @pl.when(c > 0)
            def _():
                pb_whole(g, c - 1).wait_recv()
                pb_out[group(g), :] += pb_in[group(g), :]

            pb_whole(g, c + 1).start()

        each(send)

    @pl.when(above_late)
    def _():
        for m in range(chunks):
            def rows_of(q, carry):
                rows = pl.ds(pl.multiple_of(q * step, step), step)
                part = jnp.dot(ahi[rows, :], bhi[:, lanes(m)], preferred_element_type=F32)
                part += jnp.dot(alo[rows, :], bhi[:, lanes(m)], preferred_element_type=F32)
                part += jnp.dot(ahi[rows, :], blo[:, lanes(m)], preferred_element_type=F32)
                lead = part.astype(BF)
                mhi[rows, lanes(m)] = lead
                mlo[rows, lanes(m)] = (part - lead.astype(F32)).astype(BF)
                return carry

            lax.fori_loop(0, chunks, rows_of, 0)
        ship_right(r - 1).wait_recv()

        def body(g):
            for m in range(chunks):
                pa_chunk(g, m, c - 1).wait_recv()
            value = right_a[group(g), :] - pa_in[group(g), :]
            resid[group(g), :] = value
            pair = split(value)
            r_copy(g, r - 1).start()
            for m in range(chunks):
                pb_out[group(g), lanes(m)] = product(pair, mhi, mlo, lanes(m))

        each(body)
        @pl.when(helper)
        def _():
            for k in range(direct):
                for q in range(parts):
                    d_relay(k, q).wait_recv()
                turn(h32, k * own, own, hhi, hlo, k * slot, jnp.float32(1.0))

        def send(g):
            pb_whole(g, c - 1).wait_recv()
            pb_out[group(g), :] += pb_in[group(g), :]
            for m in range(chunks):
                pb_chunk(g, m, c + 1).start()

        each(send)

        @pl.when(helper)
        def _():
            pair = split(right[...] - pb_out[...])
            for k in range(early):
                if k >= direct:
                    for q in range(parts):
                        d_relay(k, q).wait_recv()
                    turn(h32, k * own, own, hhi, hlo, k * slot, jnp.float32(1.0))
                tail[k] = product(pair, hhi, hlo, slice(k * slot, (k + 1) * slot))[:, :own]
                for h in range(2):
                    h_copy(k, h).start()

    @pl.when(works & jnp.logical_not(final) & jnp.logical_not(above_late))
    def _():
        slices()

    @pl.when(final)
    def _():
        def body(g):
            for m in range(chunks):
                pb_chunk(g, m, c - 1).wait_recv()
            pair = split(right[group(g), :] - pb_in[group(g), :])
            for k in range(early, n):
                value = product(pair, bhi, blo, slice((k - early) * slot, (k - early + 1) * slot))
                if k == n - 1:
                    out[0, group(g), :] = value[:, :own]
                else:
                    tail[k, group(g), :] = value[:, :own]
                    t_copy(k, g).start()

        each(body)

    needs = jnp.logical_not(first | works | late)

    @pl.when(needs & last_col & (r >= early))
    def _():
        for g in range(groups):
            t_copy(n - 1, g).wait_recv()

    @pl.when(needs & last_col & (r < early))
    def _():
        for h in range(2):
            h_copy(0, h).wait_recv()

    @pl.when((needs & jnp.logical_not(last_col)) | above_late)
    def _():
        s_copy(0).wait_recv()

    @pl.when(ships & jnp.logical_not(first))
    def _():
        for k in range(chunks):
            ship(k, r + 1).wait_send()

        @pl.when(c == r)
        def _():
            ship_right(r + 1).wait_send()

    x_by_group = (
        ((lax.rem(c, 2) == 0) & (first | (works & (r + 2 < n) & jnp.logical_not(above_late))))
        | (late & (r + 3 < n))
    )

    @pl.when(x_by_group)
    def _():
        for g in range(groups):
            x_whole(g, r + 1).wait_send()

    @pl.when(works & (lax.rem(c, 2) == 1) & (r + 2 < n))
    def _():
        for g in range(groups):
            for m in range(chunks):
                x_chunk(g, m, r + 1).wait_send()

    @pl.when(above_late)
    def _():
        for g in range(groups):
            r_copy(g, r - 1).wait_send()

    @pl.when(interior)
    def _():
        for g in range(groups):
            pb_whole(g, c + 1).wait_send()
            for m in range(chunks):
                pa_chunk(g, m, c + 1).wait_send()

    @pl.when(above)
    def _():
        for g in range(groups):
            for m in range(chunks):
                pb_chunk(g, m, c + 1).wait_send()

    for k in range(n):
        @pl.when(
            (works & jnp.logical_not(final) & jnp.logical_not(above) & (k < r) & ((k == r - 1) | (c == r)))
            | (late & (k < r + 2) & (k != r))
        )
        def _():
            s_copy(k).wait_send()

    @pl.when(relay)
    def _():
        for k, q in relayed:
            d_relay(k, q).wait_send()

    @pl.when(helper)
    def _():
        for k in range(early):
            for h in range(2):
                h_copy(k, h).wait_send()

    @pl.when(final)
    def _():
        for k, q in pieces:
            d_copy(k, q).wait_send()
        for k in range(early, n - 1):
            for g in range(groups):
                t_copy(k, g).wait_send()


def local(n, factor, rhs, pattern):
    size, columns = rhs.shape[1], rhs.shape[2]
    step = 256 if size % 256 == 0 else size
    chunks = size // step
    groups = 4
    own = size // n
    slot = (own + 127) // 128 * 128
    early = n // 2
    dma = pltpu.SemaphoreType.DMA
    vm = pltpu.VMEM
    wide = max(size, (n - early) * slot)
    solved = pl.pallas_call(
        functools.partial(kernel, n, size, columns, step, groups, own, slot),
        out_shape=jax.ShapeDtypeStruct((1, columns, own), F32),
        in_specs=[pl.BlockSpec(memory_space=pltpu.HBM)] * 3,
        out_specs=pl.BlockSpec(memory_space=pltpu.VMEM),
        scratch_shapes=[
            pltpu.SMEM(pattern.shape, jnp.int32),
            vm((size, size), F32), vm((size, size), F32), vm((early * own, size), F32),
            vm((size, size), BF), vm((size, size), BF),
            vm((size, wide), BF), vm((size, wide), BF),
            vm((size, size), BF), vm((size, size), BF),
            vm((size, early * slot), BF), vm((size, early * slot), BF),
            *[vm((columns, size), F32)] * 8,
            vm((n, columns, own), F32), vm((n, columns, own), F32),
            dma((chunks,)), dma, dma, dma((chunks,)), dma((chunks,)), dma, dma,
            dma((groups, chunks)), dma((groups, chunks)),
            dma((groups, chunks)), dma((groups, chunks)),
            dma((groups, chunks)), dma((groups, chunks)),
            dma((n,)), dma((groups,)), dma((n, groups)),
            dma((early, 3)), dma((early, 3)), dma((groups,)), dma((groups,)),
        ],
        compiler_params=pltpu.CompilerParams(
            collective_id=0, has_side_effects=True, vmem_limit_bytes=40 * 1024 * 1024
        ),
    )(*[pltpu.with_memory_space_constraint(v, pltpu.HBM) for v in (factor, jnp.swapaxes(rhs, 1, 2), pattern)])
    return jnp.swapaxes(solved, 1, 2)


def solution(mesh):
    in_specs = (P(("grp", "row"), "col", None, None), P(("grp", "row"), None, None), P("grp", None))
    out_specs = P(("grp", "col"), "row", None)
    return jax.shard_map(
        functools.partial(local, mesh.shape["row"]),
        mesh=mesh, in_specs=in_specs, out_specs=out_specs, check_vma=False,
    )
```

```python
import functools

import jax
import jax.numpy as jnp
from jax import lax
from jax.experimental import pallas as pl
from jax.experimental.pallas import tpu as pltpu
from jax.sharding import PartitionSpec as P

MESH = pl.DeviceIdType.MESH
BF = jnp.bfloat16
F32 = jnp.float32


def split(value):
    lead = value.astype(BF)
    rest = (value - lead.astype(F32)).astype(BF)
    return jnp.concatenate([lead, rest], axis=0), lead


def product(pair, hi, lo, cols):
    both, lead = pair
    rows = lead.shape[0]
    part = jnp.dot(both, hi[:, cols], preferred_element_type=F32)
    rest = jnp.dot(lead, lo[:, cols], preferred_element_type=F32)
    return part[:rows] + part[rows:] + rest


def turn(source, start, count, hi, lo, at, keep):
    width = 128 if count % 128 == 0 else count
    for t in range(0, count, width):
        full = source[start + t:start + t + width, :].T * keep
        lead = full.astype(BF)
        hi[:, at + t:at + t + width] = lead
        lo[:, at + t:at + t + width] = (full - lead.astype(F32)).astype(BF)


def pack(value):
    rows, width = value.shape
    if width % 128 != 64:
        return value
    body, rest = value[:, :width - 64], value[:, width - 64:]
    parts = [body[:, t:t + 128] for t in range(0, width - 64, 128)]
    return jnp.concatenate(parts + [jnp.concatenate([rest[:rows // 2], rest[rows // 2:]], axis=1)], axis=0)


def unpack(packed, rows, width):
    if width % 128 != 64:
        return packed
    count = width // 128
    parts = [packed[t * rows:(t + 1) * rows] for t in range(count)]
    rest = packed[count * rows:]
    return jnp.concatenate(parts + [jnp.concatenate([rest[:, :64], rest[:, 64:]], axis=0)], axis=1)


def packed_shape(rows, width):
    return (rows * width // 128, 128) if width % 128 == 64 else (rows, width)


def across(pair, block):
    both, lead = pair
    rows = lead.shape[0]
    dims = (((1,), (1,)), ((), ()))
    top = block.astype(BF)
    low = (block - top.astype(F32)).astype(BF)
    part = lax.dot_general(both, top, dims, preferred_element_type=F32)
    rest = lax.dot_general(lead, low, dims, preferred_element_type=F32)
    return part[:rows] + part[rows:] + rest


def kernel(
    n, size, rhs_count, step, groups, own, slot,
    factor, rhs, pattern, out,
    links, a32, b32, h32, ahi, alo, bhi, blo, mhi, mlo, hhi, hlo,
    right, right_a, xbuf, resid, pa_in, pa_out, pb_in, pb_out, piece, tail, crate, land,
    a_sem, r_sem, l_sem, ship_send, ship_recv, rb_send, rb_recv, x_send, x_recv,
    pa_send, pa_recv, pb_send, pb_recv, s_send, s_recv, t_send, d_send, d_recv, rr_send, rr_recv,
):
    r = lax.axis_index("row")
    c = lax.axis_index("col")
    chunks = size // step
    ng = rhs_count // groups
    early = n // 2
    direct = early // 2
    parts = 3 if own % 24 == 0 else 1
    third = own // parts
    half = rhs_count // 2
    odd = lax.rem(r, 2) == 1
    even = jnp.logical_not(odd)
    port = r + 1 - lax.rem(r, 2)
    first = (r == 0) & (c == 0)
    second = (r == 1) & (c == 0)
    interior = odd & (c < r - 1)
    above = odd & (c == r - 1)
    above_late = above & (r > 1)
    below = odd & (c == r)
    final = below & (r == n - 1)
    helper = above & (r == n - 1)
    below_mid = below & (r < n - 1)
    relay = (r == n - 3) & (c == n - 1)
    ships = even & (c <= r)
    late = even & (c == r) & (r > 0)
    works = odd & (c <= r)
    last_col = c == n - 1
    upstream = c > port

    def load(k):
        rows = pl.ds(k * step, step)
        return pltpu.make_async_copy(factor.at[0, 0, rows, :], a32.at[rows, :], a_sem.at[k])

    def load_right():
        return pltpu.make_async_copy(rhs.at[0], right, r_sem)

    def load_links():
        return pltpu.make_async_copy(pattern, links, l_sem)

    @pl.when(works)
    def _():
        load_links().start()

    @pl.when(first | works)
    def _():
        load_right().start()

    @pl.when(first | works | late)
    def _():
        for k in range(chunks):
            load(k).start()

    barrier = pltpu.get_barrier_semaphore()

    def hello(row, col):
        pl.semaphore_signal(barrier, inc=1, device_id={"row": row, "col": col}, device_id_type=MESH)

    @pl.when(odd & (c <= r - 1))
    def _():
        hello(r - 1, c)

    @pl.when(interior)
    def _():
        hello(jnp.where((c == r - 3) & (c > 0), r - 3, r - 2), c)

    @pl.when(works & (c > 0))
    def _():
        hello(r, c - 1)

    @pl.when(helper)
    def _():
        hello(n - 1, n - 1)
        hello(n - 3, n - 1)

    @pl.when(relay)
    def _():
        hello(n - 1, n - 1)

    @pl.when(upstream & last_col & (r < early))
    def _():
        hello(n - 1, n - 2)

    @pl.when(upstream & jnp.logical_not(last_col & (r < early)))
    def _():
        hello(c, c)

    @pl.when(even & (c <= r + 1) & jnp.logical_not(first))
    def _():
        hello(r + 1, c)

    def one_if(flag):
        return jnp.where(flag, 1, 0)

    @pl.when(ships)
    def _():
        pl.semaphore_wait(barrier, 1 + jnp.where(late, r + one_if(r + 3 < n), 0))

    def meet():
        count = one_if(jnp.logical_not(second)) + one_if((r + 2 < n) & jnp.logical_not(above_late)) + one_if(c < r)
        count += jnp.where(below_mid, r - 1, 0)
        count += jnp.where(final, n - early, 0) + jnp.where(helper, early, 0)
        pl.semaphore_wait(barrier, count)

    def ship(k, row):
        rows = pl.ds(k * step, step)
        return pltpu.make_async_remote_copy(
            src_ref=factor.at[0, 0, rows, :], dst_ref=b32.at[rows, :],
            send_sem=ship_send.at[k], recv_sem=ship_recv.at[k],
            device_id={"row": row}, device_id_type=MESH,
        )

    def ship_right(row):
        return pltpu.make_async_remote_copy(
            src_ref=rhs.at[0], dst_ref=right_a, send_sem=rb_send, recv_sem=rb_recv,
            device_id={"row": row}, device_id_type=MESH,
        )

    def group(g):
        return pl.ds(pl.multiple_of(g * ng, ng), ng)

    def lanes(m):
        return slice(m * step, (m + 1) * step)

    def x_whole(g, row):
        return pltpu.make_async_remote_copy(
            src_ref=xbuf.at[group(g), :], dst_ref=xbuf.at[group(g), :],
            send_sem=x_send.at[g, 0], recv_sem=x_recv.at[g, 0],
            device_id={"row": row}, device_id_type=MESH,
        )

    def x_chunk(g, m, row):
        return pltpu.make_async_remote_copy(
            src_ref=xbuf.at[group(g), lanes(m)], dst_ref=xbuf.at[group(g), lanes(m)],
            send_sem=x_send.at[g, m], recv_sem=x_recv.at[g, m],
            device_id={"row": row}, device_id_type=MESH,
        )

    def pa_chunk(g, m, col):
        return pltpu.make_async_remote_copy(
            src_ref=pa_out.at[group(g), lanes(m)], dst_ref=pa_in.at[group(g), lanes(m)],
            send_sem=pa_send.at[g, m], recv_sem=pa_recv.at[g, m],
            device_id={"col": col}, device_id_type=MESH,
        )

    def pb_chunk(g, m, col):
        return pltpu.make_async_remote_copy(
            src_ref=pb_out.at[group(g), lanes(m)], dst_ref=pb_in.at[group(g), lanes(m)],
            send_sem=pb_send.at[g, m], recv_sem=pb_recv.at[g, m],
            device_id={"col": col}, device_id_type=MESH,
        )

    def pb_whole(g, col):
        return pltpu.make_async_remote_copy(
            src_ref=pb_out.at[group(g), :], dst_ref=pb_in.at[group(g), :],
            send_sem=pb_send.at[g, 0], recv_sem=pb_recv.at[g, 0],
            device_id={"col": col}, device_id_type=MESH,
        )

    def s_copy(k):
        return pltpu.make_async_remote_copy(
            src_ref=piece.at[k], dst_ref=out.at[0], send_sem=s_send.at[k, 0], recv_sem=s_recv.at[0],
            device_id={"row": k}, device_id_type=MESH,
        )

    def half_copy(k, h):
        rows = slice(h * half, (h + 1) * half)
        return pltpu.make_async_remote_copy(
            src_ref=piece.at[k, rows, :], dst_ref=out.at[0, rows, :], send_sem=s_send.at[k, h], recv_sem=s_recv.at[h],
            device_id={"row": k}, device_id_type=MESH,
        )

    def h_copy(k):
        return pltpu.make_async_remote_copy(
            src_ref=crate.at[k], dst_ref=land, send_sem=t_send.at[k, 0], recv_sem=s_recv.at[0],
            device_id={"row": k, "col": n - 1}, device_id_type=MESH,
        )

    def t_copy(k, g):
        return pltpu.make_async_remote_copy(
            src_ref=tail.at[k, group(g), :], dst_ref=out.at[0, group(g), :],
            send_sem=t_send.at[k, g], recv_sem=s_recv.at[g],
            device_id={"row": k}, device_id_type=MESH,
        )

    def r_copy(g, row):
        return pltpu.make_async_remote_copy(
            src_ref=resid.at[group(g), :], dst_ref=resid.at[group(g), :],
            send_sem=rr_send.at[g], recv_sem=rr_recv.at[g],
            device_id={"row": row}, device_id_type=MESH,
        )

    def d_rows(k, q):
        return pl.ds(k * own + q * third, third)

    def d_copy(k, q):
        return pltpu.make_async_remote_copy(
            src_ref=factor.at[0, 0, d_rows(k, q), :], dst_ref=h32.at[d_rows(k, q), :],
            send_sem=d_send.at[k, q], recv_sem=d_recv.at[k, q],
            device_id={"row": n - 1 if k < direct else n - 3, "col": n - 2 if k < direct else n - 1},
            device_id_type=MESH,
        )

    def d_relay(k, q):
        return pltpu.make_async_remote_copy(
            src_ref=h32.at[d_rows(k, q), :], dst_ref=h32.at[d_rows(k, q), :],
            send_sem=d_send.at[k, q], recv_sem=d_recv.at[k, q],
            device_id={"row": n - 1, "col": n - 2}, device_id_type=MESH,
        )

    pieces = [(k, q) for k in range(early) for q in range(parts)]
    relayed = [(k, q) for k, q in pieces if k >= direct]

    def each(body):
        def step_of(g, carry):
            body(g)
            return carry

        lax.fori_loop(0, groups, step_of, 0)

    def rolled(pair, hi, lo, emit):
        before = None
        for m in range(chunks):
            part = product(pair, hi, lo, lanes(m))
            if m:
                emit(m - 1, before)
            before = part
        emit(chunks - 1, before)

    def prepare(k, hi, lo, keep):
        load(k).wait()
        turn(a32, k * step, step, hi, lo, k * step, keep)

    def receive(k, keep):
        ship(k, r - 1).wait_recv()
        turn(b32, k * step, step, ahi, alo, k * step, keep)

    def slices():
        for k in range(n):
            @pl.when((k < r) & jnp.logical_not(second) & ((k == r - 1) | (c == r)))
            def _():
                piece[k] = xbuf[:, k * own:(k + 1) * own]
                s_copy(k).start()

            @pl.when(k == r)
            def _():
                out[0] = xbuf[:, k * own:(k + 1) * own]

    @pl.when(ships & jnp.logical_not(first))
    def _():
        for k in range(chunks):
            ship(k, r + 1).start()

        @pl.when(c == r)
        def _():
            ship_right(r + 1).start()

    @pl.when(late)
    def _():
        for k in range(chunks):
            prepare(k, bhi, blo, jnp.float32(1.0))
        for h in range(2):
            rows = slice(h * half, (h + 1) * half)
            some = range(h * groups // 2, (h + 1) * groups // 2)
            for g in some:
                r_copy(g, r + 1).wait_recv()
            xbuf[rows, :] = product(split(resid[rows, :]), bhi, blo, slice(0, size))

            @pl.when(r + 3 < n)
            def _():
                for g in some:
                    x_whole(g, r + 3).start()

            for k in range(n):
                @pl.when((k < r + 2) & (k != r))
                def _():
                    piece[k, rows, :] = xbuf[rows, k * own:(k + 1) * own]
                    half_copy(k, h).start()

                @pl.when(k == r)
                def _():
                    out[0, rows, :] = xbuf[rows, k * own:(k + 1) * own]

    @pl.when(first)
    def _():
        load_right().wait()
        pair = split(right[...])
        strip = 128 if step % 128 == 0 else step
        for m in range(chunks):
            load(m).wait()
            for t in range(m * step, (m + 1) * step, strip):
                xbuf[:, t:t + strip] = across(pair, a32[t:t + strip, :])
        for g in range(groups):
            x_whole(g, 1).start()
        out[0] = xbuf[:, :own]

    @pl.when(relay)
    def _():
        pl.semaphore_wait(barrier, 1)
        for k, q in relayed:
            d_copy(k, q).wait_recv()
            d_relay(k, q).start()

    @pl.when(works)
    def _():
        load_links().wait()

        @pl.when(final)
        def _():
            meet()
            for q in range(parts):
                for k in range(early):
                    d_copy(k, q).start()

        load_right().wait()
        keep_own = jnp.where(below | (links[r, c] == 1), 1.0, 0.0).astype(F32)
        keep_up = jnp.where(above | (links[r - 1, c] == 1), 1.0, 0.0).astype(F32)

        @pl.when(jnp.logical_not(final))
        def _():
            for k in range(chunks):
                prepare(k, bhi, blo, keep_own)

        @pl.when(final)
        def _():
            for k in range(chunks):
                load(k).wait()
            for k in range(early, n):
                turn(a32, k * own, own, bhi, blo, (k - early) * slot, keep_own)

        @pl.when(interior | above_late)
        def _():
            for k in range(chunks):
                receive(k, keep_up)

        @pl.when(jnp.logical_not(final))
        def _():
            meet()

        @pl.when(second)
        def _():
            def body(g):
                x_whole(g, 0).wait_recv()
                if n > 2:
                    x_whole(g, 3).start()
                pair = split(xbuf[group(g), :])

                def emit(m, part):
                    pb_out[group(g), lanes(m)] = part
                    pb_chunk(g, m, 1).start()

                rolled(pair, bhi, blo, emit)

            each(body)

        @pl.when(below_mid)
        def _():
            def body(g):
                for m in range(chunks):
                    pb_chunk(g, m, c - 1).wait_recv()
                pair = split(right[group(g), :] - pb_in[group(g), :])

                def emit(m, part):
                    xbuf[group(g), lanes(m)] = part
                    x_chunk(g, m, r + 2).start()

                rolled(pair, bhi, blo, emit)

            each(body)

        @pl.when(interior)
        def _():
            def body(g):
                @pl.when(lax.rem(c, 2) == 0)
                def _():
                    x_whole(g, r - 2).wait_recv()

                    @pl.when(r + 2 < n)
                    def _():
                        x_whole(g, r + 2).start()

                @pl.when(lax.rem(c, 2) == 1)
                def _():
                    for m in range(chunks):
                        x_chunk(g, m, r - 2).wait_recv()

                        @pl.when(r + 2 < n)
                        def _():
                            x_chunk(g, m, r + 2).start()

                @pl.when(c > 0)
                def _():
                    for m in range(chunks):
                        pa_chunk(g, m, c - 1).wait_recv()

                pair = split(xbuf[group(g), :])

                def emit(m, part):
                    pa_out[group(g), lanes(m)] = jnp.where(c > 0, part + pa_in[group(g), lanes(m)], part)
                    pa_chunk(g, m, c + 1).start()

                rolled(pair, ahi, alo, emit)

            each(body)
            pair = split(xbuf[...])
            for m in range(chunks):
                pb_out[:, lanes(m)] = product(pair, bhi, blo, lanes(m))

            def send(g):
                @pl.when(c > 0)
                def _():
                    pb_whole(g, c - 1).wait_recv()
                    pb_out[group(g), :] += pb_in[group(g), :]

                pb_whole(g, c + 1).start()

            each(send)

        @pl.when(above_late)
        def _():
            for m in range(chunks):
                def rows_of(q, carry):
                    rows = pl.ds(pl.multiple_of(q * step, step), step)
                    part = jnp.dot(ahi[rows, :], bhi[:, lanes(m)], preferred_element_type=F32)
                    part += jnp.dot(alo[rows, :], bhi[:, lanes(m)], preferred_element_type=F32)
                    part += jnp.dot(ahi[rows, :], blo[:, lanes(m)], preferred_element_type=F32)
                    lead = part.astype(BF)
                    mhi[rows, lanes(m)] = lead
                    mlo[rows, lanes(m)] = (part - lead.astype(F32)).astype(BF)
                    return carry

                lax.fori_loop(0, chunks, rows_of, 0)
            ship_right(r - 1).wait_recv()

            def body(g):
                for m in range(chunks):
                    pa_chunk(g, m, c - 1).wait_recv()
                value = right_a[group(g), :] - pa_in[group(g), :]
                resid[group(g), :] = value
                pair = split(value)
                r_copy(g, r - 1).start()
                for m in range(chunks):
                    pb_out[group(g), lanes(m)] = product(pair, mhi, mlo, lanes(m))

            each(body)
            @pl.when(helper)
            def _():
                for k in range(direct):
                    for q in range(parts):
                        d_relay(k, q).wait_recv()
                    turn(h32, k * own, own, hhi, hlo, k * slot, jnp.float32(1.0))

            def send(g):
                pb_whole(g, c - 1).wait_recv()
                pb_out[group(g), :] += pb_in[group(g), :]
                for m in range(chunks):
                    pb_chunk(g, m, c + 1).start()

            each(send)

            @pl.when(helper)
            def _():
                pair = split(right[...] - pb_out[...])
                for k in range(early):
                    if k >= direct:
                        for q in range(parts):
                            d_relay(k, q).wait_recv()
                        turn(h32, k * own, own, hhi, hlo, k * slot, jnp.float32(1.0))
                    crate[k] = pack(product(pair, hhi, hlo, slice(k * slot, (k + 1) * slot))[:, :own])
                    h_copy(k).start()

        @pl.when(works & jnp.logical_not(final) & jnp.logical_not(above_late))
        def _():
            slices()

        @pl.when(final)
        def _():
            def body(g):
                for m in range(chunks):
                    pb_chunk(g, m, c - 1).wait_recv()
                pair = split(right[group(g), :] - pb_in[group(g), :])
                values = [
                    product(pair, bhi, blo, slice((k - early) * slot, (k - early + 1) * slot))
                    for k in range(early, n)
                ]
                for k in range(early, n - 1):
                    tail[k, group(g), :] = values[k - early][:, :own]
                    t_copy(k, g).start()
                out[0, group(g), :] = values[-1][:, :own]

            each(body)

        @pl.when(final)
        def _():
            for k, q in pieces:
                d_copy(k, q).wait_send()
            for k in range(early, n - 1):
                for g in range(groups):
                    t_copy(k, g).wait_send()

        @pl.when(above)
        def _():
            for g in range(groups):
                for m in range(chunks):
                    pb_chunk(g, m, c + 1).wait_send()

            @pl.when(r > 1)
            def _():
                for g in range(groups):
                    r_copy(g, r - 1).wait_send()
                for h in range(2):
                    half_copy(0, h).wait_recv()

            @pl.when(helper)
            def _():
                for k in range(early):
                    h_copy(k).wait_send()

        @pl.when(interior)
        def _():
            for g in range(groups):
                pb_whole(g, c + 1).wait_send()
                for m in range(chunks):
                    pa_chunk(g, m, c + 1).wait_send()

        @pl.when(r + 2 < n)
        def _():
            @pl.when((lax.rem(c, 2) == 0) & jnp.logical_not(above_late))
            def _():
                for g in range(groups):
                    x_whole(g, r + 1).wait_send()

            @pl.when(lax.rem(c, 2) == 1)
            def _():
                for g in range(groups):
                    for m in range(chunks):
                        x_chunk(g, m, r + 1).wait_send()

        @pl.when(interior | below_mid)
        def _():
            for k in range(n):
                @pl.when((k < r) & ((k == r - 1) | (c == r)))
                def _():
                    s_copy(k).wait_send()

    @pl.when(first | (late & (r + 3 < n)))
    def _():
        for g in range(groups):
            x_whole(g, r + 1).wait_send()

    @pl.when(late)
    def _():
        for k in range(n):
            @pl.when((k < r + 2) & (k != r))
            def _():
                for h in range(2):
                    half_copy(k, h).wait_send()

    @pl.when(ships & jnp.logical_not(first))
    def _():
        for k in range(chunks):
            ship(k, r + 1).wait_send()

        @pl.when(c == r)
        def _():
            ship_right(r + 1).wait_send()

    @pl.when(jnp.logical_not(first | works | late))
    def _():
        by_half = (c > 0) & (lax.rem(c, 2) == 0) & (r < c + 2)

        @pl.when(by_half)
        def _():
            for h in range(2):
                half_copy(0, h).wait_recv()

        @pl.when(jnp.logical_not(last_col | by_half))
        def _():
            s_copy(0).wait_recv()

        @pl.when(last_col)
        def _():
            @pl.when(relay)
            def _():
                for k, q in relayed:
                    d_relay(k, q).wait_send()

            @pl.when(r >= early)
            def _():
                for g in range(groups):
                    t_copy(n - 1, g).wait_recv()

            @pl.when(r < early)
            def _():
                h_copy(0).wait_recv()
                out[0] = unpack(land[...], rhs_count, own)


def local(n, factor, rhs, pattern):
    size, columns = rhs.shape[1], rhs.shape[2]
    step = 256 if size % 256 == 0 else size
    chunks = size // step
    groups = 4
    own = size // n
    slot = (own + 127) // 128 * 128
    early = n // 2
    dma = pltpu.SemaphoreType.DMA
    vm = pltpu.VMEM
    wide = max(size, (n - early) * slot)
    solved = pl.pallas_call(
        functools.partial(kernel, n, size, columns, step, groups, own, slot),
        out_shape=jax.ShapeDtypeStruct((1, columns, own), F32),
        in_specs=[pl.BlockSpec(memory_space=pltpu.HBM)] * 3,
        out_specs=pl.BlockSpec(memory_space=pltpu.VMEM),
        scratch_shapes=[
            pltpu.SMEM(pattern.shape, jnp.int32),
            vm((size, size), F32), vm((size, size), F32), vm((early * own, size), F32),
            vm((size, size), BF), vm((size, size), BF),
            vm((size, wide), BF), vm((size, wide), BF),
            vm((size, size), BF), vm((size, size), BF),
            vm((size, early * slot), BF), vm((size, early * slot), BF),
            *[vm((columns, size), F32)] * 8,
            vm((n, columns, own), F32), vm((n, columns, own), F32),
            vm((early, *packed_shape(columns, own)), F32), vm(packed_shape(columns, own), F32),
            dma((chunks,)), dma, dma, dma((chunks,)), dma((chunks,)), dma, dma,
            dma((groups, chunks)), dma((groups, chunks)),
            dma((groups, chunks)), dma((groups, chunks)),
            dma((groups, chunks)), dma((groups, chunks)),
            dma((n, 2)), dma((groups,)), dma((n, groups)),
            dma((early, 3)), dma((early, 3)), dma((groups,)), dma((groups,)),
        ],
        compiler_params=pltpu.CompilerParams(
            collective_id=0, has_side_effects=True, vmem_limit_bytes=40 * 1024 * 1024
        ),
    )(*[pltpu.with_memory_space_constraint(v, pltpu.HBM) for v in (factor, jnp.swapaxes(rhs, 1, 2), pattern)])
    return jnp.swapaxes(solved, 1, 2)


def solution(mesh):
    in_specs = (P(("grp", "row"), "col", None, None), P(("grp", "row"), None, None), P("grp", None))
    out_specs = P(("grp", "col"), "row", None)
    return jax.shard_map(
        functools.partial(local, mesh.shape["row"]),
        mesh=mesh, in_specs=in_specs, out_specs=out_specs, check_vma=False,
    )
```

```python
import functools

import jax
import jax.numpy as jnp
from jax import lax
from jax.experimental import pallas as pl
from jax.experimental.pallas import tpu as pltpu
from jax.sharding import PartitionSpec as P

MESH = pl.DeviceIdType.MESH
BF = jnp.bfloat16
F32 = jnp.float32


def split(value):
    lead = value.astype(BF)
    rest = (value - lead.astype(F32)).astype(BF)
    return jnp.concatenate([lead, rest], axis=0), lead


def product(pair, hi, lo, cols):
    both, lead = pair
    rows = lead.shape[0]
    part = jnp.dot(both, hi[:, cols], preferred_element_type=F32)
    rest = jnp.dot(lead, lo[:, cols], preferred_element_type=F32)
    return part[:rows] + part[rows:] + rest


def turn(source, start, count, hi, lo, at, keep):
    width = 128 if count % 128 == 0 else count
    for t in range(0, count, width):
        full = source[start + t:start + t + width, :].T * keep
        lead = full.astype(BF)
        hi[:, at + t:at + t + width] = lead
        lo[:, at + t:at + t + width] = (full - lead.astype(F32)).astype(BF)


def pack(value):
    rows, width = value.shape
    if width % 128 != 64:
        return value
    body, rest = value[:, :width - 64], value[:, width - 64:]
    parts = [body[:, t:t + 128] for t in range(0, width - 64, 128)]
    return jnp.concatenate(parts + [jnp.concatenate([rest[:rows // 2], rest[rows // 2:]], axis=1)], axis=0)


def unpack(packed, rows, width):
    if width % 128 != 64:
        return packed
    count = width // 128
    parts = [packed[t * rows:(t + 1) * rows] for t in range(count)]
    rest = packed[count * rows:]
    return jnp.concatenate(parts + [jnp.concatenate([rest[:, :64], rest[:, 64:]], axis=0)], axis=1)


def packed_shape(rows, width):
    return (rows * width // 128, 128) if width % 128 == 64 else (rows, width)


def across(pair, block):
    both, lead = pair
    rows = lead.shape[0]
    dims = (((1,), (1,)), ((), ()))
    top = block.astype(BF)
    low = (block - top.astype(F32)).astype(BF)
    part = lax.dot_general(both, top, dims, preferred_element_type=F32)
    rest = lax.dot_general(lead, low, dims, preferred_element_type=F32)
    return part[:rows] + part[rows:] + rest


def kernel(
    n, size, rhs_count, step, groups, own, slot,
    factor, rhs, pattern, out,
    links, a32, b32, h32, ahi, alo, bhi, blo, mhi, mlo, hhi, hlo,
    right, right_a, xbuf, resid, pa_in, pa_out, pb_in, pb_out, piece, tail, crate, land,
    a_sem, r_sem, l_sem, ship_send, ship_recv, rb_send, rb_recv, x_send, x_recv,
    pa_send, pa_recv, pb_send, pb_recv, s_send, s_recv, t_send, d_send, d_recv, rr_send, rr_recv,
):
    r = lax.axis_index("row")
    c = lax.axis_index("col")
    chunks = size // step
    ng = rhs_count // groups
    early = n // 2
    direct = early // 2
    parts = 3 if own % 24 == 0 else 1
    third = own // parts
    half = rhs_count // 2
    odd = lax.rem(r, 2) == 1
    even = jnp.logical_not(odd)
    port = r + 1 - lax.rem(r, 2)
    first = (r == 0) & (c == 0)
    second = (r == 1) & (c == 0)
    interior = odd & (c < r - 1)
    above = odd & (c == r - 1)
    above_late = above & (r > 1)
    below = odd & (c == r)
    final = below & (r == n - 1)
    helper = above & (r == n - 1)
    below_mid = below & (r < n - 1)
    relay = (r == n - 3) & (c == n - 1)
    ships = even & (c <= r)
    late = even & (c == r) & (r > 0)
    works = odd & (c <= r)
    last_col = c == n - 1
    upstream = c > port

    def load(k):
        rows = pl.ds(k * step, step)
        return pltpu.make_async_copy(factor.at[0, 0, rows, :], a32.at[rows, :], a_sem.at[k])

    def load_right():
        return pltpu.make_async_copy(rhs.at[0], right, r_sem)

    def load_links():
        return pltpu.make_async_copy(pattern, links, l_sem)

    @pl.when(works)
    def _():
        load_links().start()

    @pl.when(first | works)
    def _():
        load_right().start()

    @pl.when(first | works | late)
    def _():
        for k in range(chunks):
            load(k).start()

    barrier = pltpu.get_barrier_semaphore()

    def hello(row, col):
        pl.semaphore_signal(barrier, inc=1, device_id={"row": row, "col": col}, device_id_type=MESH)

    @pl.when(odd & (c <= r - 1))
    def _():
        hello(r - 1, c)

    @pl.when(interior)
    def _():
        hello(jnp.where((c == r - 3) & (c > 0), r - 3, r - 2), c)

    @pl.when(works & (c > 0))
    def _():
        hello(r, c - 1)

    @pl.when(helper)
    def _():
        hello(n - 1, n - 1)
        hello(n - 3, n - 1)

    @pl.when(relay)
    def _():
        hello(n - 1, n - 1)

    @pl.when(upstream & last_col & (r < early))
    def _():
        hello(n - 1, n - 2)

    @pl.when(upstream & jnp.logical_not(last_col & (r < early)))
    def _():
        hello(c, c)

    @pl.when(even & (c <= r + 1) & jnp.logical_not(first))
    def _():
        hello(r + 1, c)

    def one_if(flag):
        return jnp.where(flag, 1, 0)

    @pl.when(ships)
    def _():
        pl.semaphore_wait(barrier, 1 + jnp.where(late, r + one_if(r + 3 < n), 0))

    def meet():
        count = one_if(jnp.logical_not(second)) + one_if((r + 2 < n) & jnp.logical_not(above_late)) + one_if(c < r)
        count += jnp.where(below_mid, r - 1, 0)
        count += jnp.where(final, n - early, 0) + jnp.where(helper, early, 0)
        pl.semaphore_wait(barrier, count)

    def ship(k, row):
        rows = pl.ds(k * step, step)
        return pltpu.make_async_remote_copy(
            src_ref=factor.at[0, 0, rows, :], dst_ref=b32.at[rows, :],
            send_sem=ship_send.at[k], recv_sem=ship_recv.at[k],
            device_id={"row": row}, device_id_type=MESH,
        )

    def ship_right(row):
        return pltpu.make_async_remote_copy(
            src_ref=rhs.at[0], dst_ref=right_a, send_sem=rb_send, recv_sem=rb_recv,
            device_id={"row": row}, device_id_type=MESH,
        )

    def group(g):
        return pl.ds(pl.multiple_of(g * ng, ng), ng)

    def lanes(m):
        return slice(m * step, (m + 1) * step)

    def x_whole(g, row):
        return pltpu.make_async_remote_copy(
            src_ref=xbuf.at[group(g), :], dst_ref=xbuf.at[group(g), :],
            send_sem=x_send.at[g, 0], recv_sem=x_recv.at[g, 0],
            device_id={"row": row}, device_id_type=MESH,
        )

    def x_chunk(g, m, row):
        return pltpu.make_async_remote_copy(
            src_ref=xbuf.at[group(g), lanes(m)], dst_ref=xbuf.at[group(g), lanes(m)],
            send_sem=x_send.at[g, m], recv_sem=x_recv.at[g, m],
            device_id={"row": row}, device_id_type=MESH,
        )

    def pa_chunk(g, m, col):
        return pltpu.make_async_remote_copy(
            src_ref=pa_out.at[group(g), lanes(m)], dst_ref=pa_in.at[group(g), lanes(m)],
            send_sem=pa_send.at[g, m], recv_sem=pa_recv.at[g, m],
            device_id={"col": col}, device_id_type=MESH,
        )

    def pb_chunk(g, m, col):
        return pltpu.make_async_remote_copy(
            src_ref=pb_out.at[group(g), lanes(m)], dst_ref=pb_in.at[group(g), lanes(m)],
            send_sem=pb_send.at[g, m], recv_sem=pb_recv.at[g, m],
            device_id={"col": col}, device_id_type=MESH,
        )

    def pb_whole(g, col):
        return pltpu.make_async_remote_copy(
            src_ref=pb_out.at[group(g), :], dst_ref=pb_in.at[group(g), :],
            send_sem=pb_send.at[g, 0], recv_sem=pb_recv.at[g, 0],
            device_id={"col": col}, device_id_type=MESH,
        )

    def s_copy(k):
        return pltpu.make_async_remote_copy(
            src_ref=piece.at[k], dst_ref=out.at[0], send_sem=s_send.at[k, 0], recv_sem=s_recv.at[0],
            device_id={"row": k}, device_id_type=MESH,
        )

    def half_copy(k, h):
        rows = slice(h * half, (h + 1) * half)
        return pltpu.make_async_remote_copy(
            src_ref=piece.at[k, rows, :], dst_ref=out.at[0, rows, :], send_sem=s_send.at[k, h], recv_sem=s_recv.at[h],
            device_id={"row": k}, device_id_type=MESH,
        )

    def h_copy(k):
        return pltpu.make_async_remote_copy(
            src_ref=crate.at[k], dst_ref=land, send_sem=t_send.at[k, 0], recv_sem=s_recv.at[0],
            device_id={"row": k, "col": n - 1}, device_id_type=MESH,
        )

    def t_copy(k, g):
        return pltpu.make_async_remote_copy(
            src_ref=tail.at[k, group(g), :], dst_ref=out.at[0, group(g), :],
            send_sem=t_send.at[k, g], recv_sem=s_recv.at[g],
            device_id={"row": k}, device_id_type=MESH,
        )

    def r_copy(g, row):
        return pltpu.make_async_remote_copy(
            src_ref=resid.at[group(g), :], dst_ref=resid.at[group(g), :],
            send_sem=rr_send.at[g], recv_sem=rr_recv.at[g],
            device_id={"row": row}, device_id_type=MESH,
        )

    def d_rows(k, q):
        return pl.ds(k * own + q * third, third)

    def d_copy(k, q):
        return pltpu.make_async_remote_copy(
            src_ref=factor.at[0, 0, d_rows(k, q), :], dst_ref=h32.at[d_rows(k, q), :],
            send_sem=d_send.at[k, q], recv_sem=d_recv.at[k, q],
            device_id={"row": n - 1 if k < direct else n - 3, "col": n - 2 if k < direct else n - 1},
            device_id_type=MESH,
        )

    def d_relay(k, q):
        return pltpu.make_async_remote_copy(
            src_ref=h32.at[d_rows(k, q), :], dst_ref=h32.at[d_rows(k, q), :],
            send_sem=d_send.at[k, q], recv_sem=d_recv.at[k, q],
            device_id={"row": n - 1, "col": n - 2}, device_id_type=MESH,
        )

    pieces = [(k, q) for k in range(early) for q in range(parts)]
    relayed = [(k, q) for k, q in pieces if k >= direct]

    def each(body):
        def step_of(g, carry):
            body(g)
            return carry

        lax.fori_loop(0, groups, step_of, 0)

    def rolled(pair, hi, lo, emit, ready=None):
        before = None
        for m in range(chunks):
            part = product(pair, hi, lo, lanes(m))
            if ready and m == min(1, chunks - 1):
                ready()
            if m:
                emit(m - 1, before)
            before = part
        emit(chunks - 1, before)

    def prepare(k, hi, lo, keep):
        load(k).wait()
        turn(a32, k * step, step, hi, lo, k * step, keep)

    def receive(k, keep):
        ship(k, r - 1).wait_recv()
        turn(b32, k * step, step, ahi, alo, k * step, keep)

    def slices():
        for k in range(n):
            @pl.when((k < r) & jnp.logical_not(second) & ((k == r - 1) | (c == r)))
            def _():
                piece[k] = xbuf[:, k * own:(k + 1) * own]
                s_copy(k).start()

            @pl.when(k == r)
            def _():
                out[0] = xbuf[:, k * own:(k + 1) * own]

    @pl.when(ships & jnp.logical_not(first))
    def _():
        for k in range(chunks):
            ship(k, r + 1).start()

        @pl.when(c == r)
        def _():
            ship_right(r + 1).start()

    @pl.when(late)
    def _():
        for k in range(chunks):
            prepare(k, bhi, blo, jnp.float32(1.0))
        for h in range(2):
            rows = slice(h * half, (h + 1) * half)
            some = range(h * groups // 2, (h + 1) * groups // 2)
            for g in some:
                r_copy(g, r + 1).wait_recv()
            xbuf[rows, :] = product(split(resid[rows, :]), bhi, blo, slice(0, size))

            @pl.when(r + 3 < n)
            def _():
                for g in some:
                    x_whole(g, r + 3).start()

            for k in range(n):
                @pl.when((k < r + 2) & (k != r))
                def _():
                    piece[k, rows, :] = xbuf[rows, k * own:(k + 1) * own]
                    half_copy(k, h).start()

                @pl.when(k == r)
                def _():
                    out[0, rows, :] = xbuf[rows, k * own:(k + 1) * own]

    @pl.when(first)
    def _():
        load_right().wait()
        pair = split(right[...])
        strip = 128 if step % 128 == 0 else step
        for m in range(chunks):
            load(m).wait()
            for t in range(m * step, (m + 1) * step, strip):
                xbuf[:, t:t + strip] = across(pair, a32[t:t + strip, :])
        for g in range(groups):
            x_whole(g, 1).start()
        out[0] = xbuf[:, :own]

    @pl.when(relay)
    def _():
        pl.semaphore_wait(barrier, 1)
        for k, q in relayed:
            d_copy(k, q).wait_recv()
            d_relay(k, q).start()

    @pl.when(works)
    def _():
        load_links().wait()

        @pl.when(final)
        def _():
            meet()
            for q in range(parts):
                for k in range(early):
                    d_copy(k, q).start()

        load_right().wait()
        keep_own = jnp.where(below | (links[r, c] == 1), 1.0, 0.0).astype(F32)
        keep_up = jnp.where(above | (links[r - 1, c] == 1), 1.0, 0.0).astype(F32)

        @pl.when(jnp.logical_not(final))
        def _():
            for k in range(chunks):
                prepare(k, bhi, blo, keep_own)

        @pl.when(final)
        def _():
            for k in range(chunks):
                load(k).wait()
            for k in range(early, n):
                turn(a32, k * own, own, bhi, blo, (k - early) * slot, keep_own)

        @pl.when(interior | above_late)
        def _():
            for k in range(chunks):
                receive(k, keep_up)

        @pl.when(jnp.logical_not(final))
        def _():
            meet()

        @pl.when(second)
        def _():
            def body(g):
                x_whole(g, 0).wait_recv()
                if n > 2:
                    x_whole(g, 3).start()
                pair = split(xbuf[group(g), :])

                def emit(m, part):
                    pb_out[group(g), lanes(m)] = part
                    pb_chunk(g, m, 1).start()

                rolled(pair, bhi, blo, emit)

            each(body)

        @pl.when(below_mid)
        def _():
            def body(g):
                for m in range(chunks):
                    pb_chunk(g, m, c - 1).wait_recv()
                pair = split(right[group(g), :] - pb_in[group(g), :])

                def emit(m, part):
                    xbuf[group(g), lanes(m)] = part
                    x_chunk(g, m, r + 2).start()

                rolled(pair, bhi, blo, emit)

            each(body)

        @pl.when(interior)
        def _():
            def body(g):
                @pl.when(lax.rem(c, 2) == 0)
                def _():
                    x_whole(g, r - 2).wait_recv()

                    @pl.when(r + 2 < n)
                    def _():
                        x_whole(g, r + 2).start()

                @pl.when(lax.rem(c, 2) == 1)
                def _():
                    for m in range(chunks):
                        x_chunk(g, m, r - 2).wait_recv()

                        @pl.when(r + 2 < n)
                        def _():
                            x_chunk(g, m, r + 2).start()

                def ready():
                    @pl.when(c > 0)
                    def _():
                        for m in range(chunks):
                            pa_chunk(g, m, c - 1).wait_recv()

                pair = split(xbuf[group(g), :])

                def emit(m, part):
                    pa_out[group(g), lanes(m)] = jnp.where(c > 0, part + pa_in[group(g), lanes(m)], part)
                    pa_chunk(g, m, c + 1).start()

                rolled(pair, ahi, alo, emit, ready)

            each(body)
            pair = split(xbuf[...])
            for m in range(chunks):
                pb_out[:, lanes(m)] = product(pair, bhi, blo, lanes(m))

            def send(g):
                @pl.when(c > 0)
                def _():
                    pb_whole(g, c - 1).wait_recv()
                    pb_out[group(g), :] += pb_in[group(g), :]

                pb_whole(g, c + 1).start()

            each(send)

        @pl.when(above_late)
        def _():
            for m in range(chunks):
                def rows_of(q, carry):
                    rows = pl.ds(pl.multiple_of(q * step, step), step)
                    part = jnp.dot(ahi[rows, :], bhi[:, lanes(m)], preferred_element_type=F32)
                    part += jnp.dot(alo[rows, :], bhi[:, lanes(m)], preferred_element_type=F32)
                    part += jnp.dot(ahi[rows, :], blo[:, lanes(m)], preferred_element_type=F32)
                    lead = part.astype(BF)
                    mhi[rows, lanes(m)] = lead
                    mlo[rows, lanes(m)] = (part - lead.astype(F32)).astype(BF)
                    return carry

                lax.fori_loop(0, chunks, rows_of, 0)
            ship_right(r - 1).wait_recv()

            def body(g):
                for m in range(chunks):
                    pa_chunk(g, m, c - 1).wait_recv()
                value = right_a[group(g), :] - pa_in[group(g), :]
                resid[group(g), :] = value
                pair = split(value)
                r_copy(g, r - 1).start()
                for m in range(chunks):
                    pb_out[group(g), lanes(m)] = product(pair, mhi, mlo, lanes(m))

            each(body)
            @pl.when(helper)
            def _():
                for k in range(direct):
                    for q in range(parts):
                        d_relay(k, q).wait_recv()
                    turn(h32, k * own, own, hhi, hlo, k * slot, jnp.float32(1.0))

            def send(g):
                pb_whole(g, c - 1).wait_recv()
                pb_out[group(g), :] += pb_in[group(g), :]
                for m in range(chunks):
                    pb_chunk(g, m, c + 1).start()

            each(send)

            @pl.when(helper)
            def _():
                pair = split(right[...] - pb_out[...])
                for k in range(early):
                    if k >= direct:
                        for q in range(parts):
                            d_relay(k, q).wait_recv()
                        turn(h32, k * own, own, hhi, hlo, k * slot, jnp.float32(1.0))
                    crate[k] = pack(product(pair, hhi, hlo, slice(k * slot, (k + 1) * slot))[:, :own])
                    h_copy(k).start()

        @pl.when(works & jnp.logical_not(final) & jnp.logical_not(above_late))
        def _():
            slices()

        @pl.when(final)
        def _():
            def body(g):
                for m in range(chunks):
                    pb_chunk(g, m, c - 1).wait_recv()
                pair = split(right[group(g), :] - pb_in[group(g), :])
                values = [
                    product(pair, bhi, blo, slice((k - early) * slot, (k - early + 1) * slot))
                    for k in range(early, n)
                ]
                for k in range(early, n - 1):
                    tail[k, group(g), :] = values[k - early][:, :own]
                    t_copy(k, g).start()
                out[0, group(g), :] = values[-1][:, :own]

            each(body)

        @pl.when(final)
        def _():
            for k, q in pieces:
                d_copy(k, q).wait_send()
            for k in range(early, n - 1):
                for g in range(groups):
                    t_copy(k, g).wait_send()

        @pl.when(above)
        def _():
            for g in range(groups):
                for m in range(chunks):
                    pb_chunk(g, m, c + 1).wait_send()

            @pl.when(r > 1)
            def _():
                for g in range(groups):
                    r_copy(g, r - 1).wait_send()
                for h in range(2):
                    half_copy(0, h).wait_recv()

            @pl.when(helper)
            def _():
                for k in range(early):
                    h_copy(k).wait_send()

        @pl.when(interior)
        def _():
            for g in range(groups):
                pb_whole(g, c + 1).wait_send()
                for m in range(chunks):
                    pa_chunk(g, m, c + 1).wait_send()

        @pl.when(r + 2 < n)
        def _():
            @pl.when((lax.rem(c, 2) == 0) & jnp.logical_not(above_late))
            def _():
                for g in range(groups):
                    x_whole(g, r + 1).wait_send()

            @pl.when(lax.rem(c, 2) == 1)
            def _():
                for g in range(groups):
                    for m in range(chunks):
                        x_chunk(g, m, r + 1).wait_send()

        @pl.when(interior | below_mid)
        def _():
            for k in range(n):
                @pl.when((k < r) & ((k == r - 1) | (c == r)))
                def _():
                    s_copy(k).wait_send()

    @pl.when(first | (late & (r + 3 < n)))
    def _():
        for g in range(groups):
            x_whole(g, r + 1).wait_send()

    @pl.when(late)
    def _():
        for k in range(n):
            @pl.when((k < r + 2) & (k != r))
            def _():
                for h in range(2):
                    half_copy(k, h).wait_send()

    @pl.when(ships & jnp.logical_not(first))
    def _():
        for k in range(chunks):
            ship(k, r + 1).wait_send()

        @pl.when(c == r)
        def _():
            ship_right(r + 1).wait_send()

    @pl.when(jnp.logical_not(first | works | late))
    def _():
        by_half = (c > 0) & (lax.rem(c, 2) == 0) & (r < c + 2)

        @pl.when(by_half)
        def _():
            for h in range(2):
                half_copy(0, h).wait_recv()

        @pl.when(jnp.logical_not(last_col | by_half))
        def _():
            s_copy(0).wait_recv()

        @pl.when(last_col)
        def _():
            @pl.when(relay)
            def _():
                for k, q in relayed:
                    d_relay(k, q).wait_send()

            @pl.when(r >= early)
            def _():
                for g in range(groups):
                    t_copy(n - 1, g).wait_recv()

            @pl.when(r < early)
            def _():
                h_copy(0).wait_recv()
                out[0] = unpack(land[...], rhs_count, own)


def local(n, factor, rhs, pattern):
    size, columns = rhs.shape[1], rhs.shape[2]
    step = 256 if size % 256 == 0 else size
    chunks = size // step
    groups = 4
    own = size // n
    slot = (own + 127) // 128 * 128
    early = n // 2
    dma = pltpu.SemaphoreType.DMA
    vm = pltpu.VMEM
    wide = max(size, (n - early) * slot)
    solved = pl.pallas_call(
        functools.partial(kernel, n, size, columns, step, groups, own, slot),
        out_shape=jax.ShapeDtypeStruct((1, columns, own), F32),
        in_specs=[pl.BlockSpec(memory_space=pltpu.HBM)] * 3,
        out_specs=pl.BlockSpec(memory_space=pltpu.VMEM),
        scratch_shapes=[
            pltpu.SMEM(pattern.shape, jnp.int32),
            vm((size, size), F32), vm((size, size), F32), vm((early * own, size), F32),
            vm((size, size), BF), vm((size, size), BF),
            vm((size, wide), BF), vm((size, wide), BF),
            vm((size, size), BF), vm((size, size), BF),
            vm((size, early * slot), BF), vm((size, early * slot), BF),
            *[vm((columns, size), F32)] * 8,
            vm((n, columns, own), F32), vm((n, columns, own), F32),
            vm((early, *packed_shape(columns, own)), F32), vm(packed_shape(columns, own), F32),
            dma((chunks,)), dma, dma, dma((chunks,)), dma((chunks,)), dma, dma,
            dma((groups, chunks)), dma((groups, chunks)),
            dma((groups, chunks)), dma((groups, chunks)),
            dma((groups, chunks)), dma((groups, chunks)),
            dma((n, 2)), dma((groups,)), dma((n, groups)),
            dma((early, 3)), dma((early, 3)), dma((groups,)), dma((groups,)),
        ],
        compiler_params=pltpu.CompilerParams(
            collective_id=0, has_side_effects=True, vmem_limit_bytes=40 * 1024 * 1024
        ),
    )(*[pltpu.with_memory_space_constraint(v, pltpu.HBM) for v in (factor, jnp.swapaxes(rhs, 1, 2), pattern)])
    return jnp.swapaxes(solved, 1, 2)


def solution(mesh):
    in_specs = (P(("grp", "row"), "col", None, None), P(("grp", "row"), None, None), P("grp", None))
    out_specs = P(("grp", "col"), "row", None)
    return jax.shard_map(
        functools.partial(local, mesh.shape["row"]),
        mesh=mesh, in_specs=in_specs, out_specs=out_specs, check_vma=False,
    )
```

```python
import functools

import jax
import jax.numpy as jnp
from jax import lax
from jax.experimental import pallas as pl
from jax.experimental.pallas import tpu as pltpu
from jax.sharding import PartitionSpec as P

MESH = pl.DeviceIdType.MESH
BF = jnp.bfloat16
F32 = jnp.float32


def split(value):
    lead = value.astype(BF)
    rest = (value - lead.astype(F32)).astype(BF)
    return jnp.concatenate([lead, rest], axis=0), lead


def product(pair, hi, lo, cols):
    both, lead = pair
    rows = lead.shape[0]
    part = jnp.dot(both, hi[:, cols], preferred_element_type=F32)
    rest = jnp.dot(lead, lo[:, cols], preferred_element_type=F32)
    return part[:rows] + part[rows:] + rest


def turn(source, start, count, hi, lo, at, keep):
    width = 128 if count % 128 == 0 else count
    for t in range(0, count, width):
        full = source[start + t:start + t + width, :].T * keep
        lead = full.astype(BF)
        hi[:, at + t:at + t + width] = lead
        lo[:, at + t:at + t + width] = (full - lead.astype(F32)).astype(BF)


def pack(value):
    rows, width = value.shape
    if width % 128 != 64:
        return value
    body, rest = value[:, :width - 64], value[:, width - 64:]
    parts = [body[:, t:t + 128] for t in range(0, width - 64, 128)]
    return jnp.concatenate(parts + [jnp.concatenate([rest[:rows // 2], rest[rows // 2:]], axis=1)], axis=0)


def unpack(packed, rows, width):
    if width % 128 != 64:
        return packed
    count = width // 128
    parts = [packed[t * rows:(t + 1) * rows] for t in range(count)]
    rest = packed[count * rows:]
    return jnp.concatenate(parts + [jnp.concatenate([rest[:, :64], rest[:, 64:]], axis=0)], axis=1)


def packed_shape(rows, width):
    return (rows * width // 128, 128) if width % 128 == 64 else (rows, width)


def across(pair, block):
    both, lead = pair
    rows = lead.shape[0]
    dims = (((1,), (1,)), ((), ()))
    top = block.astype(BF)
    low = (block - top.astype(F32)).astype(BF)
    part = lax.dot_general(both, top, dims, preferred_element_type=F32)
    rest = lax.dot_general(lead, low, dims, preferred_element_type=F32)
    return part[:rows] + part[rows:] + rest


def kernel(
    n, size, rhs_count, step, groups, own, slot,
    factor, rhs, pattern, out,
    links, a32, b32, h32, ahi, alo, bhi, blo, mhi, mlo, hhi, hlo,
    right, right_a, xbuf, resid, pa_in, pa_out, pb_in, pb_out, piece, tail, crate, land,
    a_sem, r_sem, l_sem, ship_send, ship_recv, rb_send, rb_recv, x_send, x_recv,
    pa_send, pa_recv, pb_send, pb_recv, s_send, s_recv, t_send, d_send, d_recv, rr_send, rr_recv,
):
    r = lax.axis_index("row")
    c = lax.axis_index("col")
    chunks = size // step
    ng = rhs_count // groups
    early = n // 2
    direct = early // 2
    parts = 3 if own % 24 == 0 else 1
    third = own // parts
    half = rhs_count // 2
    odd = lax.rem(r, 2) == 1
    even = jnp.logical_not(odd)
    port = r + 1 - lax.rem(r, 2)
    first = (r == 0) & (c == 0)
    second = (r == 1) & (c == 0)
    interior = odd & (c < r - 1)
    above = odd & (c == r - 1)
    above_late = above & (r > 1)
    below = odd & (c == r)
    final = below & (r == n - 1)
    helper = above & (r == n - 1)
    below_mid = below & (r < n - 1)
    relay = (r == n - 3) & (c == n - 1)
    ships = even & (c <= r)
    late = even & (c == r) & (r > 0)
    works = odd & (c <= r)
    last_col = c == n - 1
    upstream = c > port

    def load(k):
        rows = pl.ds(k * step, step)
        return pltpu.make_async_copy(factor.at[0, 0, rows, :], a32.at[rows, :], a_sem.at[k])

    def load_right():
        return pltpu.make_async_copy(rhs.at[0], right, r_sem)

    def load_links():
        return pltpu.make_async_copy(pattern, links, l_sem)

    @pl.when(works)
    def _():
        load_links().start()

    @pl.when(first | works)
    def _():
        load_right().start()

    @pl.when(first | works | late)
    def _():
        for k in range(chunks):
            load(k).start()

    barrier = pltpu.get_barrier_semaphore()

    def hello(row, col):
        pl.semaphore_signal(barrier, inc=1, device_id={"row": row, "col": col}, device_id_type=MESH)

    @pl.when(odd & (c <= r - 1))
    def _():
        hello(r - 1, c)

    @pl.when(interior)
    def _():
        hello(jnp.where((c == r - 3) & (c > 0), r - 3, r - 2), c)

    @pl.when(works & (c > 0))
    def _():
        hello(r, c - 1)

    @pl.when(helper)
    def _():
        hello(n - 1, n - 1)
        hello(n - 3, n - 1)

    @pl.when(relay)
    def _():
        hello(n - 1, n - 1)

    @pl.when(upstream & last_col & (r < early))
    def _():
        hello(n - 1, n - 2)

    @pl.when(upstream & jnp.logical_not(last_col & (r < early)))
    def _():
        hello(c, c)

    @pl.when(even & (c <= r + 1) & jnp.logical_not(first))
    def _():
        hello(r + 1, c)

    def one_if(flag):
        return jnp.where(flag, 1, 0)

    @pl.when(ships)
    def _():
        pl.semaphore_wait(barrier, 1 + jnp.where(late, r + one_if(r + 3 < n), 0))

    def meet():
        count = one_if(jnp.logical_not(second)) + one_if((r + 2 < n) & jnp.logical_not(above_late)) + one_if(c < r)
        count += jnp.where(below_mid, r - 1, 0)
        count += jnp.where(final, n - early, 0) + jnp.where(helper, early, 0)
        pl.semaphore_wait(barrier, count)

    def ship(k, row):
        rows = pl.ds(k * step, step)
        return pltpu.make_async_remote_copy(
            src_ref=factor.at[0, 0, rows, :], dst_ref=b32.at[rows, :],
            send_sem=ship_send.at[k], recv_sem=ship_recv.at[k],
            device_id={"row": row}, device_id_type=MESH,
        )

    def ship_right(row):
        return pltpu.make_async_remote_copy(
            src_ref=rhs.at[0], dst_ref=right_a, send_sem=rb_send, recv_sem=rb_recv,
            device_id={"row": row}, device_id_type=MESH,
        )

    def group(g):
        return pl.ds(pl.multiple_of(g * ng, ng), ng)

    def lanes(m):
        return slice(m * step, (m + 1) * step)

    def x_whole(g, row):
        return pltpu.make_async_remote_copy(
            src_ref=xbuf.at[group(g), :], dst_ref=xbuf.at[group(g), :],
            send_sem=x_send.at[g, 0], recv_sem=x_recv.at[g, 0],
            device_id={"row": row}, device_id_type=MESH,
        )

    def x_chunk(g, m, row):
        return pltpu.make_async_remote_copy(
            src_ref=xbuf.at[group(g), lanes(m)], dst_ref=xbuf.at[group(g), lanes(m)],
            send_sem=x_send.at[g, m], recv_sem=x_recv.at[g, m],
            device_id={"row": row}, device_id_type=MESH,
        )

    def pa_chunk(g, m, col):
        return pltpu.make_async_remote_copy(
            src_ref=pa_out.at[group(g), lanes(m)], dst_ref=pa_in.at[group(g), lanes(m)],
            send_sem=pa_send.at[g, m], recv_sem=pa_recv.at[g, m],
            device_id={"col": col}, device_id_type=MESH,
        )

    def pb_chunk(g, m, col):
        return pltpu.make_async_remote_copy(
            src_ref=pb_out.at[group(g), lanes(m)], dst_ref=pb_in.at[group(g), lanes(m)],
            send_sem=pb_send.at[g, m], recv_sem=pb_recv.at[g, m],
            device_id={"col": col}, device_id_type=MESH,
        )

    def pb_whole(g, col):
        return pltpu.make_async_remote_copy(
            src_ref=pb_out.at[group(g), :], dst_ref=pb_in.at[group(g), :],
            send_sem=pb_send.at[g, 0], recv_sem=pb_recv.at[g, 0],
            device_id={"col": col}, device_id_type=MESH,
        )

    def s_copy(k):
        return pltpu.make_async_remote_copy(
            src_ref=piece.at[k], dst_ref=out.at[0], send_sem=s_send.at[k, 0], recv_sem=s_recv.at[0],
            device_id={"row": k}, device_id_type=MESH,
        )

    def half_copy(k, h):
        rows = slice(h * half, (h + 1) * half)
        return pltpu.make_async_remote_copy(
            src_ref=piece.at[k, rows, :], dst_ref=out.at[0, rows, :], send_sem=s_send.at[k, h], recv_sem=s_recv.at[h],
            device_id={"row": k}, device_id_type=MESH,
        )

    def h_copy(k):
        return pltpu.make_async_remote_copy(
            src_ref=crate.at[k], dst_ref=land, send_sem=t_send.at[k, 0], recv_sem=s_recv.at[0],
            device_id={"row": k, "col": n - 1}, device_id_type=MESH,
        )

    def t_copy(k, g):
        return pltpu.make_async_remote_copy(
            src_ref=tail.at[k, group(g), :], dst_ref=out.at[0, group(g), :],
            send_sem=t_send.at[k, g], recv_sem=s_recv.at[g],
            device_id={"row": k}, device_id_type=MESH,
        )

    def r_copy(g, row):
        return pltpu.make_async_remote_copy(
            src_ref=resid.at[group(g), :], dst_ref=resid.at[group(g), :],
            send_sem=rr_send.at[g], recv_sem=rr_recv.at[g],
            device_id={"row": row}, device_id_type=MESH,
        )

    def d_rows(k, q):
        return pl.ds(k * own + q * third, third)

    def d_copy(k, q):
        return pltpu.make_async_remote_copy(
            src_ref=factor.at[0, 0, d_rows(k, q), :], dst_ref=h32.at[d_rows(k, q), :],
            send_sem=d_send.at[k, q], recv_sem=d_recv.at[k, q],
            device_id={"row": n - 1 if k < direct else n - 3, "col": n - 2 if k < direct else n - 1},
            device_id_type=MESH,
        )

    def d_relay(k, q):
        return pltpu.make_async_remote_copy(
            src_ref=h32.at[d_rows(k, q), :], dst_ref=h32.at[d_rows(k, q), :],
            send_sem=d_send.at[k, q], recv_sem=d_recv.at[k, q],
            device_id={"row": n - 1, "col": n - 2}, device_id_type=MESH,
        )

    pieces = [(k, q) for k in range(early) for q in range(parts)]
    relayed = [(k, q) for k, q in pieces if k >= direct]

    def each(body):
        def step_of(g, carry):
            body(g)
            return carry

        lax.fori_loop(0, groups, step_of, 0)

    def rolled(pair, hi, lo, emit):
        before = None
        for m in range(chunks):
            part = product(pair, hi, lo, lanes(m))
            if m:
                emit(m - 1, before)
            before = part
        emit(chunks - 1, before)

    def prepare(k, hi, lo, keep):
        load(k).wait()
        turn(a32, k * step, step, hi, lo, k * step, keep)

    def receive(k, keep):
        ship(k, r - 1).wait_recv()
        turn(b32, k * step, step, ahi, alo, k * step, keep)

    def slices():
        for k in range(n):
            @pl.when((k < r) & jnp.logical_not(second) & ((k == r - 1) | (c == r)))
            def _():
                piece[k] = xbuf[:, k * own:(k + 1) * own]
                s_copy(k).start()

            @pl.when(k == r)
            def _():
                out[0] = xbuf[:, k * own:(k + 1) * own]

    @pl.when(ships & jnp.logical_not(first))
    def _():
        for k in range(chunks):
            ship(k, r + 1).start()

        @pl.when(c == r)
        def _():
            ship_right(r + 1).start()

    @pl.when(late)
    def _():
        for k in range(chunks):
            prepare(k, bhi, blo, jnp.float32(1.0))
        for h in range(2):
            rows = slice(h * half, (h + 1) * half)
            some = range(h * groups // 2, (h + 1) * groups // 2)
            for g in some:
                r_copy(g, r + 1).wait_recv()
            xbuf[rows, :] = product(split(resid[rows, :]), bhi, blo, slice(0, size))

            @pl.when(r + 3 < n)
            def _():
                for g in some:
                    x_whole(g, r + 3).start()

            for k in range(n):
                @pl.when((k < r + 2) & (k != r))
                def _():
                    piece[k, rows, :] = xbuf[rows, k * own:(k + 1) * own]
                    half_copy(k, h).start()

                @pl.when(k == r)
                def _():
                    out[0, rows, :] = xbuf[rows, k * own:(k + 1) * own]

    @pl.when(first)
    def _():
        load_right().wait()
        pair = split(right[...])
        strip = 128 if step % 128 == 0 else step
        for m in range(chunks):
            load(m).wait()
            for t in range(m * step, (m + 1) * step, strip):
                xbuf[:, t:t + strip] = across(pair, a32[t:t + strip, :])
        for g in range(groups):
            x_whole(g, 1).start()
        out[0] = xbuf[:, :own]

    @pl.when(relay)
    def _():
        pl.semaphore_wait(barrier, 1)
        for k, q in relayed:
            d_copy(k, q).wait_recv()
            d_relay(k, q).start()

    @pl.when(works)
    def _():
        load_links().wait()

        @pl.when(final)
        def _():
            meet()
            for q in range(parts):
                for k in range(early):
                    d_copy(k, q).start()

        load_right().wait()
        keep_own = jnp.where(below | (links[r, c] == 1), 1.0, 0.0).astype(F32)
        keep_up = jnp.where(above | (links[r - 1, c] == 1), 1.0, 0.0).astype(F32)

        @pl.when(jnp.logical_not(final))
        def _():
            for k in range(chunks):
                prepare(k, bhi, blo, keep_own)

        @pl.when(final)
        def _():
            for k in range(chunks):
                load(k).wait()
            for k in range(early, n):
                turn(a32, k * own, own, bhi, blo, (k - early) * slot, keep_own)

        @pl.when(interior | above_late)
        def _():
            for k in range(chunks):
                receive(k, keep_up)

        @pl.when(jnp.logical_not(final))
        def _():
            meet()

        @pl.when(second)
        def _():
            def body(g):
                x_whole(g, 0).wait_recv()
                if n > 2:
                    x_whole(g, 3).start()
                pair = split(xbuf[group(g), :])

                def emit(m, part):
                    pb_out[group(g), lanes(m)] = part
                    pb_chunk(g, m, 1).start()

                rolled(pair, bhi, blo, emit)

            each(body)

        @pl.when(below_mid)
        def _():
            def body(g):
                def got():
                    for m in range(chunks):
                        pb_chunk(g, m, c - 1).wait_recv()

                if n > 4:
                    pl.when(r == 1)(got)

                    @pl.when(r > 1)
                    def _():
                        pb_whole(g, c - 1).wait_recv()
                else:
                    got()
                pair = split(right[group(g), :] - pb_in[group(g), :])

                def emit(m, part):
                    xbuf[group(g), lanes(m)] = part
                    x_chunk(g, m, r + 2).start()

                rolled(pair, bhi, blo, emit)

            each(body)

        @pl.when(interior)
        def _():
            def body(g):
                @pl.when(lax.rem(c, 2) == 0)
                def _():
                    x_whole(g, r - 2).wait_recv()

                    @pl.when(r + 2 < n)
                    def _():
                        x_whole(g, r + 2).start()

                @pl.when(lax.rem(c, 2) == 1)
                def _():
                    for m in range(chunks):
                        x_chunk(g, m, r - 2).wait_recv()

                        @pl.when(r + 2 < n)
                        def _():
                            x_chunk(g, m, r + 2).start()

                @pl.when(c > 0)
                def _():
                    for m in range(chunks):
                        pa_chunk(g, m, c - 1).wait_recv()

                pair = split(xbuf[group(g), :])

                def emit(m, part):
                    pa_out[group(g), lanes(m)] = jnp.where(c > 0, part + pa_in[group(g), lanes(m)], part)
                    pa_chunk(g, m, c + 1).start()

                rolled(pair, ahi, alo, emit)

            each(body)
            pair = split(xbuf[...])
            for m in range(chunks):
                pb_out[:, lanes(m)] = product(pair, bhi, blo, lanes(m))

            def send(g):
                @pl.when(c > 0)
                def _():
                    pb_whole(g, c - 1).wait_recv()
                    pb_out[group(g), :] += pb_in[group(g), :]

                pb_whole(g, c + 1).start()

            each(send)

        @pl.when(above_late)
        def _():
            for m in range(chunks):
                def rows_of(q, carry):
                    rows = pl.ds(pl.multiple_of(q * step, step), step)
                    part = jnp.dot(ahi[rows, :], bhi[:, lanes(m)], preferred_element_type=F32)
                    part += jnp.dot(alo[rows, :], bhi[:, lanes(m)], preferred_element_type=F32)
                    part += jnp.dot(ahi[rows, :], blo[:, lanes(m)], preferred_element_type=F32)
                    lead = part.astype(BF)
                    mhi[rows, lanes(m)] = lead
                    mlo[rows, lanes(m)] = (part - lead.astype(F32)).astype(BF)
                    return carry

                lax.fori_loop(0, chunks, rows_of, 0)
            ship_right(r - 1).wait_recv()

            def body(g):
                for m in range(chunks):
                    pa_chunk(g, m, c - 1).wait_recv()
                value = right_a[group(g), :] - pa_in[group(g), :]
                resid[group(g), :] = value
                pair = split(value)
                r_copy(g, r - 1).start()
                for m in range(chunks):
                    pb_out[group(g), lanes(m)] = product(pair, mhi, mlo, lanes(m))

            each(body)
            @pl.when(helper)
            def _():
                for k in range(direct):
                    for q in range(parts):
                        d_relay(k, q).wait_recv()
                    turn(h32, k * own, own, hhi, hlo, k * slot, jnp.float32(1.0))

            def send(g):
                pb_whole(g, c - 1).wait_recv()
                pb_out[group(g), :] += pb_in[group(g), :]
                pb_whole(g, c + 1).start()

            each(send)

            @pl.when(helper)
            def _():
                pair = split(right[...] - pb_out[...])
                for k in range(early):
                    if k >= direct:
                        for q in range(parts):
                            d_relay(k, q).wait_recv()
                        turn(h32, k * own, own, hhi, hlo, k * slot, jnp.float32(1.0))
                    crate[k] = pack(product(pair, hhi, hlo, slice(k * slot, (k + 1) * slot))[:, :own])
                    h_copy(k).start()

        @pl.when(works & jnp.logical_not(final) & jnp.logical_not(above_late))
        def _():
            slices()

        @pl.when(final)
        def _():
            def body(g):
                pb_whole(g, c - 1).wait_recv()
                pair = split(right[group(g), :] - pb_in[group(g), :])
                values = [
                    product(pair, bhi, blo, slice((k - early) * slot, (k - early + 1) * slot))
                    for k in range(early, n)
                ]
                for k in range(early, n - 1):
                    tail[k, group(g), :] = values[k - early][:, :own]
                    t_copy(k, g).start()
                out[0, group(g), :] = values[-1][:, :own]

            each(body)

        @pl.when(final)
        def _():
            for k, q in pieces:
                d_copy(k, q).wait_send()
            for k in range(early, n - 1):
                for g in range(groups):
                    t_copy(k, g).wait_send()

        @pl.when(above)
        def _():
            @pl.when(r == 1)
            def _():
                for g in range(groups):
                    for m in range(chunks):
                        pb_chunk(g, m, c + 1).wait_send()

            @pl.when(r > 1)
            def _():
                for g in range(groups):
                    pb_whole(g, c + 1).wait_send()
                    r_copy(g, r - 1).wait_send()
                for h in range(2):
                    half_copy(0, h).wait_recv()

            @pl.when(helper)
            def _():
                for k in range(early):
                    h_copy(k).wait_send()

        @pl.when(interior)
        def _():
            for g in range(groups):
                pb_whole(g, c + 1).wait_send()
                for m in range(chunks):
                    pa_chunk(g, m, c + 1).wait_send()

        @pl.when(r + 2 < n)
        def _():
            @pl.when((lax.rem(c, 2) == 0) & jnp.logical_not(above_late))
            def _():
                for g in range(groups):
                    x_whole(g, r + 1).wait_send()

            @pl.when(lax.rem(c, 2) == 1)
            def _():
                for g in range(groups):
                    for m in range(chunks):
                        x_chunk(g, m, r + 1).wait_send()

        @pl.when(interior | below_mid)
        def _():
            for k in range(n):
                @pl.when((k < r) & ((k == r - 1) | (c == r)))
                def _():
                    s_copy(k).wait_send()

    @pl.when(first | (late & (r + 3 < n)))
    def _():
        for g in range(groups):
            x_whole(g, r + 1).wait_send()

    @pl.when(late)
    def _():
        for k in range(n):
            @pl.when((k < r + 2) & (k != r))
            def _():
                for h in range(2):
                    half_copy(k, h).wait_send()

    @pl.when(ships & jnp.logical_not(first))
    def _():
        for k in range(chunks):
            ship(k, r + 1).wait_send()

        @pl.when(c == r)
        def _():
            ship_right(r + 1).wait_send()

    @pl.when(jnp.logical_not(first | works | late))
    def _():
        by_half = (c > 0) & (lax.rem(c, 2) == 0) & (r < c + 2)

        @pl.when(by_half)
        def _():
            for h in range(2):
                half_copy(0, h).wait_recv()

        @pl.when(jnp.logical_not(last_col | by_half))
        def _():
            s_copy(0).wait_recv()

        @pl.when(last_col)
        def _():
            @pl.when(relay)
            def _():
                for k, q in relayed:
                    d_relay(k, q).wait_send()

            @pl.when(r >= early)
            def _():
                for g in range(groups):
                    t_copy(n - 1, g).wait_recv()

            @pl.when(r < early)
            def _():
                h_copy(0).wait_recv()
                out[0] = unpack(land[...], rhs_count, own)


def local(n, factor, rhs, pattern):
    size, columns = rhs.shape[1], rhs.shape[2]
    step = 256 if size % 256 == 0 else size
    chunks = size // step
    groups = 4
    own = size // n
    slot = (own + 127) // 128 * 128
    early = n // 2
    dma = pltpu.SemaphoreType.DMA
    vm = pltpu.VMEM
    wide = max(size, (n - early) * slot)
    solved = pl.pallas_call(
        functools.partial(kernel, n, size, columns, step, groups, own, slot),
        out_shape=jax.ShapeDtypeStruct((1, columns, own), F32),
        in_specs=[pl.BlockSpec(memory_space=pltpu.HBM)] * 3,
        out_specs=pl.BlockSpec(memory_space=pltpu.VMEM),
        scratch_shapes=[
            pltpu.SMEM(pattern.shape, jnp.int32),
            vm((size, size), F32), vm((size, size), F32), vm((early * own, size), F32),
            vm((size, size), BF), vm((size, size), BF),
            vm((size, wide), BF), vm((size, wide), BF),
            vm((size, size), BF), vm((size, size), BF),
            vm((size, early * slot), BF), vm((size, early * slot), BF),
            *[vm((columns, size), F32)] * 8,
            vm((n, columns, own), F32), vm((n, columns, own), F32),
            vm((early, *packed_shape(columns, own)), F32), vm(packed_shape(columns, own), F32),
            dma((chunks,)), dma, dma, dma((chunks,)), dma((chunks,)), dma, dma,
            dma((groups, chunks)), dma((groups, chunks)),
            dma((groups, chunks)), dma((groups, chunks)),
            dma((groups, chunks)), dma((groups, chunks)),
            dma((n, 2)), dma((groups,)), dma((n, groups)),
            dma((early, 3)), dma((early, 3)), dma((groups,)), dma((groups,)),
        ],
        compiler_params=pltpu.CompilerParams(
            collective_id=0, has_side_effects=True, vmem_limit_bytes=40 * 1024 * 1024
        ),
    )(*[pltpu.with_memory_space_constraint(v, pltpu.HBM) for v in (factor, jnp.swapaxes(rhs, 1, 2), pattern)])
    return jnp.swapaxes(solved, 1, 2)


def solution(mesh):
    in_specs = (P(("grp", "row"), "col", None, None), P(("grp", "row"), None, None), P("grp", None))
    out_specs = P(("grp", "col"), "row", None)
    return jax.shard_map(
        functools.partial(local, mesh.shape["row"]),
        mesh=mesh, in_specs=in_specs, out_specs=out_specs, check_vma=False,
    )
```
